32 devices in a mesh: groups: 2 (over x), frame: 16 (over z, y, core).
Axes of the slice: x: 2, y: 2, z: 4, core: 2. Of those that a mesh axis runs over, the one named last changes fastest.
Arguments:
- video_qkv: bfloat16 [3, 32, 128, 1536], P(None, ('groups', 'frame')), parts along dimension 1, may hold values from -8 to 8
- text_qkv: bfloat16 [3, 512, 1536], P(None, ('groups', 'frame')), parts along dimension 1, may hold values from -8 to 8
- head_kind: int32 [24], P('groups'), parts along dimension 0, may hold values from 0 to 1, as said below
- text_len: int32 [2], P('groups'), parts along dimension 0, may hold values from 64 to 256
Outputs:
- video_out: bfloat16 [32, 128, 1536], P(('groups', 'frame')), parts along dimension 0
- text_out: bfloat16 [512, 1536], P(('groups', 'frame')), parts along dimension 0
The draws below stay inside these ranges and needn't reach their ends.
There are 2 independent parts, one for each index of `groups`. The reference program is written for one: setup_inputs(seed, part) draws one part's arguments, and reference() takes and returns one part's arrays. A program takes and returns all parts, laid end to end along the dimension named above; each array names one. Nothing has to cross between parts.
Inputs may be any that keep to these rules, and one draw needn't show every extreme that they name: `head_kind`: exactly 6 of the 12 entries are 1.
All inputs are finite; a program needn't handle non-finite values.
Results may differ from the reference program's by a relative error of at most 0.009.
Values may be sent and summed in bfloat16 or wider, within the bound.
A program may use at most 448 MiB of HBM per device.

```python
import jax
import jax.numpy as jnp
from jax import lax

H = 12
HD = 128
TXT = 256
P_SIZE = 128
FRAMES = 16
HT = 6


def rough_values(key, full_shape):
    base_key = jax.random.fold_in(key, 11)
    drawn = jnp.clip(jax.random.normal(base_key, full_shape, jnp.float32), -6.0, 6.0)
    return drawn


def draw_video_qkv(key, part):
    full_shape = (3, FRAMES, P_SIZE, H * HD)
    drawn = rough_values(jax.random.fold_in(key, 21), full_shape)
    return drawn.astype(jnp.bfloat16)


def draw_text_qkv(key, part):
    full_shape = (3, TXT, H * HD)
    drawn = rough_values(jax.random.fold_in(key, 31), full_shape)
    return drawn.astype(jnp.bfloat16)


def draw_head_kind(key, part):
    shuffled = jax.random.permutation(jax.random.fold_in(key, 3), H)
    return (shuffled < HT).astype(jnp.int32)


def setup_inputs(seed: int = 0, part: int = 0) -> dict:
    key_of = jax.random.split(jax.random.key(seed), 5)
    part_splits = jax.random.split(jax.random.fold_in(key_of[4], part), 5)
    video_qkv = draw_video_qkv(jax.random.fold_in(jax.random.fold_in(key_of[4], part), 71), part)
    text_qkv = draw_text_qkv(jax.random.fold_in(jax.random.fold_in(key_of[4], part), 71), part)
    head_kind = draw_head_kind(jax.random.fold_in(jax.random.fold_in(key_of[4], part), 71), part)
    text_len = jax.random.randint(part_splits[3], (1,), TXT // 4, TXT + 1).astype(jnp.int32)
    return {"video_qkv": video_qkv, "text_qkv": text_qkv, "head_kind": head_kind, "text_len": text_len}


masked_score = -1e30


def reference(video_qkv, text_qkv, head_kind, text_len):
    video = video_qkv.reshape(3, FRAMES, P_SIZE, H, HD)
    texts = text_qkv.reshape(3, TXT, H, HD)
    score_scale = HD ** -0.5
    text_valid = jnp.arange(TXT) < text_len[0]
    spatial_heads = jnp.nonzero(head_kind == 0, size=H - HT)[0].astype(jnp.int32)
    temporal_heads = jnp.nonzero(head_kind == 1, size=HT)[0].astype(jnp.int32)
    video_spatial = jnp.take(video, spatial_heads, axis=3)
    text_spatial = jnp.take(texts, spatial_heads, axis=2)
    text_keys_sp = text_spatial[1].astype(jnp.float32)
    text_values_sp = text_spatial[2].astype(jnp.float32)

    def spatial_frame(frame_block):
        queries = frame_block[0].astype(jnp.float32)
        own_scores = jnp.einsum("phd,khd->hpk", queries, frame_block[1].astype(jnp.float32)) * score_scale
        text_scores = jnp.einsum("phd,khd->hpk", queries, text_keys_sp) * score_scale
        text_scores = jnp.where(text_valid, text_scores, masked_score)
        row_max = jnp.maximum(own_scores.max(-1), text_scores.max(-1))[..., None]
        own_exp = jnp.exp(own_scores - row_max)
        text_exp = jnp.exp(text_scores - row_max)
        totals = own_exp.sum(-1) + text_exp.sum(-1)
        own_weight = lax.optimization_barrier(own_exp.astype(jnp.bfloat16)).astype(jnp.float32)
        text_weight = lax.optimization_barrier(text_exp.astype(jnp.bfloat16)).astype(jnp.float32)
        summed = jnp.einsum("hpk,khd->phd", own_weight, frame_block[2].astype(jnp.float32))
        summed = summed + jnp.einsum("hpk,khd->phd", text_weight, text_values_sp)
        return summed / totals.T[..., None]

    spatial_out = lax.map(spatial_frame, jnp.moveaxis(video_spatial, 1, 0))
    video_temporal = jnp.moveaxis(jnp.take(video, temporal_heads, axis=3), 3, 0)

    def temporal_head(head_block):
        queries = head_block[0].astype(jnp.float32)
        scores = jnp.einsum("fpd,gpd->pfg", queries, head_block[1].astype(jnp.float32)) * score_scale
        row_max = scores.max(-1, keepdims=True)
        exps = jnp.exp(scores - row_max)
        totals = exps.sum(-1)
        weight = lax.optimization_barrier(exps.astype(jnp.bfloat16)).astype(jnp.float32)
        summed = jnp.einsum("pfg,gpd->fpd", weight, head_block[2].astype(jnp.float32))
        return summed / totals.T[..., None]

    temporal_out = jnp.moveaxis(lax.map(temporal_head, video_temporal), 0, 2)
    joined = jnp.concatenate([spatial_out, temporal_out], axis=2)
    order = jnp.concatenate([spatial_heads, temporal_heads]).astype(jnp.int32)
    inverse = jnp.argsort(order).astype(jnp.int32)
    video_out = jnp.take(joined, inverse, axis=2).astype(jnp.bfloat16).reshape(FRAMES, P_SIZE, H * HD)

    flat_keys = video[1].reshape(FRAMES * P_SIZE, H, HD)
    flat_values = video[2].reshape(FRAMES * P_SIZE, H, HD)

    def text_head(head_index):
        queries = texts[0][:, head_index]
        text_scores = jnp.dot(queries, texts[1][:, head_index].T, preferred_element_type=jnp.float32) * score_scale
        text_scores = jnp.where(text_valid, text_scores, masked_score)
        video_scores = jnp.dot(queries, flat_keys[:, head_index].T, preferred_element_type=jnp.float32) * score_scale
        row_max = jnp.maximum(text_scores.max(-1), video_scores.max(-1))[:, None]
        text_exp = jnp.exp(text_scores - row_max)
        video_exp = jnp.exp(video_scores - row_max)
        totals = text_exp.sum(-1) + video_exp.sum(-1)
        summed = jnp.dot(text_exp.astype(jnp.bfloat16), texts[2][:, head_index], preferred_element_type=jnp.float32)
        summed = summed + jnp.dot(video_exp.astype(jnp.bfloat16), flat_values[:, head_index], preferred_element_type=jnp.float32)
        return summed / totals[:, None]

    text_all = lax.map(text_head, jnp.arange(H, dtype=jnp.int32))
    text_out = jnp.moveaxis(text_all, 0, 1).astype(jnp.bfloat16).reshape(TXT, H * HD)
    return video_out, text_out
```

```python
import functools

import jax
import jax.numpy as jnp
import numpy as np
from jax import lax
from jax.experimental import pallas as pl
from jax.experimental.pallas import tpu as pltpu
from jax.sharding import PartitionSpec as P

masked_score = -1e30
log2_e = float(np.log2(np.e))
f32 = jnp.float32
bf16 = jnp.bfloat16


def pick(one_hot, array, dims):
    return jnp.einsum(dims, one_hot, array, preferred_element_type=f32).astype(bf16)


def plain_body(video_qkv, text_qkv, head_kind, text_len):
    head_count = head_kind.shape[0]
    head_width = video_qkv.shape[-1]
    head_dim = head_width // head_count
    positions = video_qkv.shape[2]
    shard_text = text_qkv.shape[1]
    half = head_count // 2
    score_scale = head_dim ** (-0.5)
    device_rank = lax.axis_index("frame")
    local_video = video_qkv.reshape(3, 1, positions, head_count, head_dim)
    gathered = lax.all_gather(text_qkv, "frame", axis=1, tiled=True)
    text_total = gathered.shape[1]
    all_text = gathered.reshape(3, text_total, head_count, head_dim)
    text_valid = jnp.arange(text_total) < text_len[0]
    head_at = jnp.arange(head_count)
    earlier = head_at[None, :] < head_at[:, None]
    same_kind = head_kind[None, :] == head_kind[:, None]
    rank = jnp.sum(jnp.where(earlier & same_kind, 1, 0), axis=1)
    place = rank + half * head_kind
    slots = (place[None, :] == head_at[:, None]).astype(bf16)
    spatial, temporal = slots[:half], slots[half:]
    own_frame = pick(spatial, local_video[:, 0], "ih,tphd->tpid")
    text_spatial = pick(spatial, all_text[1:], "ih,tphd->tpid")
    joint_keys = jnp.concatenate([own_frame[1], text_spatial[0]], axis=0)
    joint_values = jnp.concatenate([own_frame[2], text_spatial[1]], axis=0)
    joint_valid = jnp.concatenate([jnp.ones((positions,), bool), text_valid])
    spatial_scores = (
        jnp.einsum("phd,khd->hpk", own_frame[0], joint_keys, preferred_element_type=f32)
        * score_scale
    )
    spatial_scores = jnp.where(joint_valid, spatial_scores, masked_score)
    row_max = spatial_scores.max(-1, keepdims=True)
    spatial_exp = jnp.exp(spatial_scores - row_max)
    totals = spatial_exp.sum(-1)
    summed = jnp.einsum(
        "hpk,khd->phd", spatial_exp.astype(bf16), joint_values, preferred_element_type=f32
    )
    spatial_result = (summed / totals.T[..., None]).astype(bf16)
    selected = pick(temporal, local_video, "ih,tfphd->tfpid")
    block = lax.all_to_all(selected, "frame", split_axis=2, concat_axis=1, tiled=True)
    scores = (
        jnp.einsum("fphd,gphd->phfg", block[0], block[1], preferred_element_type=f32) * score_scale
    )
    block_max = scores.max(-1, keepdims=True)
    exps = jnp.exp(scores - block_max)
    block_totals = exps.sum(-1)
    block_sum = jnp.einsum(
        "phfg,gphd->fphd", exps.astype(bf16), block[2], preferred_element_type=f32
    )
    result = (block_sum / jnp.transpose(block_totals, (2, 0, 1))[..., None]).astype(bf16)
    temporal_result = lax.all_to_all(result, "frame", split_axis=0, concat_axis=1, tiled=True)[0]
    joined = jnp.concatenate([spatial_result, temporal_result], axis=1)
    video_out = pick(slots, joined, "ih,pid->phd").reshape(1, positions, head_width)
    text_queries = all_text[0]
    own_text = text_qkv.reshape(3, shard_text, head_count, head_dim)
    own_valid = device_rank * shard_text + jnp.arange(shard_text) < text_len[0]
    local_keys = jnp.concatenate([local_video[1, 0], own_text[1]], axis=0)
    local_values = jnp.concatenate([local_video[2, 0], own_text[2]], axis=0)
    local_valid = jnp.concatenate([jnp.ones((positions,), bool), own_valid])
    query_scores = (
        jnp.einsum("thd,khd->thk", text_queries, local_keys, preferred_element_type=f32)
        * score_scale
    )
    query_scores = jnp.where(local_valid, query_scores, masked_score)
    local_max = query_scores.max(-1)
    global_max = lax.pmax(local_max, "frame")
    query_exp = jnp.exp(query_scores - global_max[..., None])
    query_totals = query_exp.sum(-1)
    query_sums = jnp.einsum(
        "thk,khd->thd", query_exp.astype(bf16), local_values, preferred_element_type=f32
    )
    query_sums = lax.psum_scatter(query_sums, "frame", scatter_dimension=0, tiled=True)
    query_totals = lax.psum_scatter(query_totals, "frame", scatter_dimension=0, tiled=True)
    text_out = (query_sums / query_totals[..., None]).astype(bf16).reshape(shard_text, head_width)
    return (video_out, text_out)


def dot_nt(a, b):
    return lax.dot_general(a, b, (((1,), (1,)), ((), ())), preferred_element_type=f32)


def dot_nn(a, b):
    return lax.dot_general(a, b, (((1,), (0,)), ((), ())), preferred_element_type=f32)


def attend(q, keys, values, ok, scale):
    s = jnp.where(ok, dot_nt(q, keys), masked_score)
    top = s.max(-1, keepdims=True)
    w = jnp.exp2((s - top) * scale).astype(bf16)
    hd = values.shape[1]
    both = dot_nn(w, jnp.concatenate([values, jnp.ones_like(values)], axis=1))
    return top, both[:, hd:], both[:, :hd]


def remote(src, dst, send_sem, recv_sem, peer):
    return pltpu.make_async_remote_copy(
        src_ref=src,
        dst_ref=dst,
        send_sem=send_sem,
        recv_sem=recv_sem,
        device_id={"frame": peer},
        device_id_type=pl.DeviceIdType.MESH,
    )


names = (
    "pair_video",
    "pair_text",
    "q_far",
    "q_first",
    "q_second",
    "kv_far",
    "kv_first",
    "kv_second",
    "kv_row",
    "kv_core",
    "part",
    "part_far",
    "attended",
    "temporal0",
    "temporal1",
    "temporal2",
)
sem_at = {name: i for i, name in enumerate(names)}


def kernel(
    heads,
    kind_hbm,
    len_hbm,
    video_hbm,
    text_hbm,
    video_out,
    text_out,
    kind_ref,
    len_ref,
    video_ref,
    text_ref,
    pair_video,
    pair_text,
    q_all,
    kv_all,
    t_send,
    t_recv,
    o_send,
    o_recv,
    p_send,
    p_recv,
    p_out,
    p_far,
    result,
    in_sem,
    send_sem,
    recv_sem,
):
    n = 16
    half = heads // 2
    third = half // 2
    positions, hd = video_ref.shape[2:]
    shard = text_ref.shape[2]
    width = heads * hd
    owned = positions // 8
    scale = hd ** (-0.5) * log2_e
    me = lax.axis_index("frame")
    core = lax.rem(me, 2)
    y = lax.rem(me // 2, 2)
    z = me // 4
    u = lax.rem(me // 2, 4)
    zh = me // 8
    chip = me // 2
    far = lax.rem(me + 8, n)
    z_near = z + 1 - 2 * lax.rem(z, 2)
    z_far = lax.rem(z + 2, 4)
    near = z_near * 4 + y * 2 + core
    across = me + 2 - 4 * y
    partner = me + 1 - 2 * core

    barrier = pltpu.get_barrier_semaphore()

    def greet(k, c):
        pl.semaphore_signal(
            barrier,
            inc=1,
            device_id={"frame": lax.rem(me + k, n)},
            device_id_type=pl.DeviceIdType.MESH,
        )
        return c

    pltpu.make_async_copy(kind_hbm, kind_ref, in_sem.at[0]).start()
    pltpu.make_async_copy(len_hbm, len_ref, in_sem.at[1]).start()
    for src, dst, i in ((text_hbm, text_ref, 2), (video_hbm, video_ref, 3)):
        for h in range(heads):
            hs = slice(h * hd, (h + 1) * hd)
            pltpu.make_async_copy(src.at[:, :, hs], dst.at[:, h], in_sem.at[i]).start()
    lax.fori_loop(1, n, greet, 0)
    for i, ref in enumerate((kind_ref, len_ref, text_ref)):
        pltpu.make_async_copy(ref, ref, in_sem.at[i]).wait()

    seen = [jnp.int32(0), jnp.int32(0)]
    places = []
    for h in range(heads):
        kind = kind_ref[h]
        places.append(jnp.where(kind == 0, seen[0], half + seen[1]))
        seen[0] = seen[0] + jnp.where(kind == 0, 1, 0)
        seen[1] = seen[1] + jnp.where(kind == 0, 0, 1)

    def head_of(i):
        first = i % half
        head = jnp.int32(first)
        for h in range(first + 1, first + half + 1):
            head = jnp.where(places[h] == i, h, head)
        return head

    head_in = [head_of(i) for i in range(heads)]

    for i in range(half):
        for t in range(2):
            kv_all[core, y, z, t, :, i * hd : (i + 1) * hd] = text_ref[t + 1, head_in[i]]
    for h in range(heads):
        q_all[u, zh, :, h * hd : (h + 1) * hd] = text_ref[0, h]

    def start(name, src, dst, to):
        i = sem_at[name]
        remote(src, dst, send_sem.at[i], recv_sem.at[i], to).start()

    def keep(name, src, dst):
        pltpu.make_async_copy(src, dst, recv_sem.at[sem_at[name]]).start()

    def landed(name, like):
        i = sem_at[name]
        remote(like, like, send_sem.at[i], recv_sem.at[i], partner).wait_recv()

    def sent(name, like):
        i = sem_at[name]
        remote(like, like, send_sem.at[i], recv_sem.at[i], partner).wait_send()

    def to_peers(name, block_of):
        def go(k, c):
            v = lax.rem(u + k, 4)
            src, dst = block_of(v)
            start(name, src, dst, zh * 8 + v * 2 + core)
            return c

        lax.fori_loop(1, 4, go, 0)

    pl.semaphore_wait(barrier, n - 1)

    mine = q_all.at[u, zh]
    start("q_far", mine, mine, far)
    to_peers("q_first", lambda v: (mine, mine))
    kv_mine = kv_all.at[core, y, z]
    start("kv_far", kv_mine, kv_mine, far)
    start("kv_first", kv_mine, kv_mine, near)
    start("pair_video", video_hbm.at[1:3], pair_video, partner)
    start("pair_text", text_hbm.at[1:3], pair_text, partner)

    pltpu.make_async_copy(video_ref, video_ref, in_sem.at[3]).wait()

    def pack(i):
        for k in range(2):
            head = head_in[half + third * k + i]
            for t in range(3):
                block = video_ref[t, head].reshape(8, owned, hd)
                t_send[i, :, k, t] = block

    def start_t(i):
        name = f"temporal{i}"
        keep(name, t_send.at[i, chip, core], t_recv.at[i, me])

        def go(k, c):
            to = lax.rem(me + k, n)
            start(name, t_send.at[i, to // 2, lax.rem(to, 2)], t_recv.at[i, me], to)
            return c

        lax.fori_loop(1, n, go, 0)

    pack(0)
    start_t(0)
    pack(1)
    pack(2)

    landed("q_far", mine)
    relayed = q_all.at[u, 1 - zh]
    to_peers("q_second", lambda v: (relayed, relayed))
    landed("kv_far", kv_mine)
    kv_relayed = kv_all.at[core, y, z_far]
    start("kv_second", kv_relayed, kv_relayed, near)
    start_t(1)

    landed("q_first", q_all.at[0:3, 0])
    landed("q_second", q_all.at[0:3, 0])
    landed("pair_video", pair_video)
    landed("pair_text", pair_text)

    length = len_ref[0]
    key = lax.broadcasted_iota(jnp.int32, (1, 2 * positions + 2 * shard), 1)
    offset = key - 2 * positions
    token = jnp.where(offset < shard, me * shard + offset, partner * shard + offset - shard)
    key_ok = (offset < 0) | (token < length)
    rows = 8 * shard
    lane = lax.broadcasted_iota(jnp.int32, (rows, 128), 1)
    tops = jnp.zeros((rows, 128), f32)
    sums = jnp.ones((rows, 128), f32)
    for h in range(heads):
        hs = slice(h * hd, (h + 1) * hd)
        q = q_all[:, :, :, hs].reshape(rows, hd)
        keys, values = (
            jnp.concatenate(
                [video_ref[t + 1, h], pair_video[t, :, hs], text_ref[t + 1, h], pair_text[t, :, hs]],
                axis=0,
            )
            for t in range(2)
        )
        top, total, summed = attend(q, keys, values, key_ok, scale)
        p_send[:, :, :, hs] = (summed / total).astype(bf16).reshape(4, 2, shard, hd)
        tops = jnp.where(lane == h, top, tops)
        sums = jnp.where(lane == h, total, sums)

    def coded(logs):
        at = lax.broadcasted_iota(jnp.int32, logs.shape, 1)
        high = logs.astype(bf16).astype(f32)
        middle = (logs - high).astype(bf16).astype(f32)
        low = logs - high - middle
        return jnp.where(
            at < 16, high, jnp.where(at < 32, pltpu.roll(middle, 16, 1), pltpu.roll(low, 32, 1))
        ).astype(bf16)

    def decoded(code):
        code = code.astype(f32)
        return code + pltpu.roll(code, 112, 1) + pltpu.roll(code, 96, 1)

    p_send[:, :, :, width:] = coded(tops * scale + jnp.log(sums) * log2_e).reshape(4, 2, shard, 128)
    keep("part", p_send.at[u], p_recv.at[u])
    to_peers("part", lambda v: (p_send.at[v], p_recv.at[u]))
    start_t(2)

    landed("kv_first", kv_mine)
    landed("kv_second", kv_mine)
    column = kv_all.at[core, y]
    start("kv_row", column, column, across)

    row_at = lax.rem(lax.broadcasted_iota(jnp.int32, (n * owned, n * owned), 0), owned)
    col_at = lax.rem(lax.broadcasted_iota(jnp.int32, (n * owned, n * owned), 1), owned)
    same = row_at == col_at

    def temporal(i):
        landed(f"temporal{i}", t_recv.at[i])
        q, k_, v = (t_recv[i, :, t].reshape(n * owned, hd) for t in range(3))
        _, total, summed = attend(q, k_, v, same, scale)
        o_send[i] = (summed / total).astype(bf16).reshape(n, owned, hd)
        dst = o_recv.at[third * core + i, chip]
        keep("attended", o_send.at[i, me], dst)

        def go(k, c):
            to = lax.rem(me + k, n)
            start("attended", o_send.at[i, to], dst, to)
            return c

        lax.fori_loop(1, n, go, 0)

    temporal(0)
    temporal(1)

    def combine(parts):
        logs = [decoded(p[:, width:]) for p in parts]
        best = functools.reduce(jnp.maximum, logs)
        weights = [jnp.exp2(jnp.minimum(log - best, 0.0)) for log in logs]
        total = functools.reduce(jnp.add, weights)
        weights = [w / total for w in weights]
        blocks = []
        for h in range(heads):
            hs = slice(h * hd, (h + 1) * hd)
            terms = [w[:, h : h + 1] * p[:, hs].astype(f32) for w, p in zip(weights, parts)]
            blocks.append(functools.reduce(jnp.add, terms).astype(bf16))
        return blocks, best + jnp.log(total) * log2_e

    landed("part", p_recv)
    blocks, logs = combine([p_recv[v, 1 - zh] for v in range(4)])
    for h in range(heads):
        p_out[:, h * hd : (h + 1) * hd] = blocks[h]
    p_out[:, width:] = coded(logs)
    start("part_far", p_out, p_far, far)

    landed("kv_row", column)
    ours = kv_all.at[core]
    start("kv_core", ours, ours, partner)

    temporal(2)

    landed("kv_core", ours)
    at = lax.broadcasted_iota(jnp.int32, (1, positions + n * shard), 1) - positions
    block = jnp.maximum(at, 0) // shard
    source = lax.rem(block, 4) * 4 + lax.rem(block // 4, 2) * 2 + block // 8
    joint_ok = (at < 0) | (source * shard + lax.rem(jnp.maximum(at, 0), shard) < length)
    for i in range(half):
        hs = slice(i * hd, (i + 1) * hd)
        keys, values = (
            jnp.concatenate(
                [video_ref[t + 1, head_in[i]], kv_all[:, :, :, t, :, hs].reshape(n * shard, hd)],
                axis=0,
            )
            for t in range(2)
        )
        _, total, summed = attend(video_ref[0, head_in[i]], keys, values, joint_ok, scale)
        result[i] = (summed / total).astype(bf16)

    landed("part_far", p_out)
    blocks, _ = combine([p_recv[v, zh] for v in range(4)] + [p_far[...]])
    for h in range(heads):
        text_out[:, h * hd : (h + 1) * hd] = blocks[h]

    landed("attended", o_recv)
    for h in range(heads):
        spatial = result[jnp.minimum(places[h], half - 1)]
        temporal_block = o_recv[jnp.maximum(places[h] - half, 0)].reshape(positions, hd)
        video_out[:, h * hd : (h + 1) * hd] = jnp.where(places[h] < half, spatial, temporal_block)

    sent("pair_video", pair_video)
    sent("pair_text", pair_text)
    sent("q_far", mine)
    sent("q_first", q_all.at[0:3, 0])
    sent("q_second", q_all.at[0:3, 0])
    sent("kv_far", kv_mine)
    sent("kv_first", kv_mine)
    sent("kv_second", kv_mine)
    sent("kv_row", column)
    sent("kv_core", ours)
    sent("part", p_send.at[0:3])
    sent("part_far", p_out)
    for i in range(3):
        sent(f"temporal{i}", t_recv.at[i, 0 : n - 1])
    sent("attended", o_send.at[:, 0 : n - 1])


def fused_body(video_qkv, text_qkv, head_kind, text_len):
    heads = head_kind.shape[0]
    _, _, positions, width = video_qkv.shape
    shard = text_qkv.shape[1]
    n, half, hd = 16, heads // 2, width // heads
    owned, narrow, coded = positions // 8, half * hd, width + 128
    vmem = pl.BlockSpec(memory_space=pltpu.VMEM)
    hbm = pl.BlockSpec(memory_space=pltpu.HBM)
    dma = pltpu.SemaphoreType.DMA
    video_out, text_out = pl.pallas_call(
        functools.partial(kernel, heads),
        out_shape=(
            jax.ShapeDtypeStruct((positions, width), bf16),
            jax.ShapeDtypeStruct((shard, width), bf16),
        ),
        in_specs=[hbm] * 4,
        out_specs=(vmem, vmem),
        scratch_shapes=[
            pltpu.SMEM((heads,), jnp.int32),
            pltpu.SMEM((1,), jnp.int32),
            pltpu.VMEM((3, heads, positions, hd), bf16),
            pltpu.VMEM((3, heads, shard, hd), bf16),
            pltpu.VMEM((2, positions, width), bf16),
            pltpu.VMEM((2, shard, width), bf16),
            pltpu.VMEM((4, 2, shard, width), bf16),
            pltpu.VMEM((2, 2, 4, 2, shard, narrow), bf16),
            pltpu.VMEM((3, 8, 2, 3, owned, hd), bf16),
            pltpu.VMEM((3, n, 3, owned, hd), bf16),
            pltpu.VMEM((3, n, owned, hd), bf16),
            pltpu.VMEM((half, 8, owned, hd), bf16),
            pltpu.VMEM((4, 2, shard, coded), bf16),
            pltpu.VMEM((4, 2, shard, coded), bf16),
            pltpu.VMEM((shard, coded), bf16),
            pltpu.VMEM((shard, coded), bf16),
            pltpu.VMEM((half, positions, hd), bf16),
            dma((4,)),
            dma((len(names),)),
            dma((len(names),)),
        ],
        compiler_params=pltpu.CompilerParams(
            collective_id=0, has_side_effects=True, vmem_limit_bytes=63 << 20
        ),
    )(head_kind, text_len, video_qkv.reshape(3, positions, width), text_qkv)
    return video_out.reshape(1, positions, width), text_out


def body(n, video_qkv, text_qkv, head_kind, text_len):
    heads = head_kind.shape[0]
    positions, width = video_qkv.shape[2:]
    shard = text_qkv.shape[1]
    whole_tiles = (
        video_qkv.shape[1] == 1
        and n == 16
        and heads == 12
        and shard % 16 == 0
        and positions % 128 == 0
        and width == heads * 128
    )
    if whole_tiles:
        return fused_body(video_qkv, text_qkv, head_kind, text_len)
    return plain_body(video_qkv, text_qkv, head_kind, text_len)


def solution(mesh):
    in_specs = (
        P(None, ("groups", "frame"), None, None),
        P(None, ("groups", "frame"), None),
        P("groups"),
        P("groups"),
    )
    out_specs = (P(("groups", "frame"), None, None), P(("groups", "frame"), None))
    return jax.shard_map(
        functools.partial(body, mesh.shape["frame"]),
        mesh=mesh,
        in_specs=in_specs,
        out_specs=out_specs,
        check_vma=False,
    )
```

```python
import functools

import jax
import jax.numpy as jnp
import numpy as np
from jax import lax
from jax.experimental import pallas as pl
from jax.experimental.pallas import tpu as pltpu
from jax.sharding import PartitionSpec as P

masked_score = -1e30
log2_e = float(np.log2(np.e))
f32 = jnp.float32
bf16 = jnp.bfloat16


def pick(one_hot, array, dims):
    return jnp.einsum(dims, one_hot, array, preferred_element_type=f32).astype(bf16)


def plain_body(video_qkv, text_qkv, head_kind, text_len):
    head_count = head_kind.shape[0]
    head_width = video_qkv.shape[-1]
    head_dim = head_width // head_count
    positions = video_qkv.shape[2]
    shard_text = text_qkv.shape[1]
    half = head_count // 2
    score_scale = head_dim ** (-0.5)
    device_rank = lax.axis_index("frame")
    local_video = video_qkv.reshape(3, 1, positions, head_count, head_dim)
    gathered = lax.all_gather(text_qkv, "frame", axis=1, tiled=True)
    text_total = gathered.shape[1]
    all_text = gathered.reshape(3, text_total, head_count, head_dim)
    text_valid = jnp.arange(text_total) < text_len[0]
    head_at = jnp.arange(head_count)
    earlier = head_at[None, :] < head_at[:, None]
    same_kind = head_kind[None, :] == head_kind[:, None]
    rank = jnp.sum(jnp.where(earlier & same_kind, 1, 0), axis=1)
    place = rank + half * head_kind
    slots = (place[None, :] == head_at[:, None]).astype(bf16)
    spatial, temporal = slots[:half], slots[half:]
    own_frame = pick(spatial, local_video[:, 0], "ih,tphd->tpid")
    text_spatial = pick(spatial, all_text[1:], "ih,tphd->tpid")
    joint_keys = jnp.concatenate([own_frame[1], text_spatial[0]], axis=0)
    joint_values = jnp.concatenate([own_frame[2], text_spatial[1]], axis=0)
    joint_valid = jnp.concatenate([jnp.ones((positions,), bool), text_valid])
    spatial_scores = (
        jnp.einsum("phd,khd->hpk", own_frame[0], joint_keys, preferred_element_type=f32)
        * score_scale
    )
    spatial_scores = jnp.where(joint_valid, spatial_scores, masked_score)
    row_max = spatial_scores.max(-1, keepdims=True)
    spatial_exp = jnp.exp(spatial_scores - row_max)
    totals = spatial_exp.sum(-1)
    summed = jnp.einsum(
        "hpk,khd->phd", spatial_exp.astype(bf16), joint_values, preferred_element_type=f32
    )
    spatial_result = (summed / totals.T[..., None]).astype(bf16)
    selected = pick(temporal, local_video, "ih,tfphd->tfpid")
    block = lax.all_to_all(selected, "frame", split_axis=2, concat_axis=1, tiled=True)
    scores = (
        jnp.einsum("fphd,gphd->phfg", block[0], block[1], preferred_element_type=f32) * score_scale
    )
    block_max = scores.max(-1, keepdims=True)
    exps = jnp.exp(scores - block_max)
    block_totals = exps.sum(-1)
    block_sum = jnp.einsum(
        "phfg,gphd->fphd", exps.astype(bf16), block[2], preferred_element_type=f32
    )
    result = (block_sum / jnp.transpose(block_totals, (2, 0, 1))[..., None]).astype(bf16)
    temporal_result = lax.all_to_all(result, "frame", split_axis=0, concat_axis=1, tiled=True)[0]
    joined = jnp.concatenate([spatial_result, temporal_result], axis=1)
    video_out = pick(slots, joined, "ih,pid->phd").reshape(1, positions, head_width)
    text_queries = all_text[0]
    own_text = text_qkv.reshape(3, shard_text, head_count, head_dim)
    own_valid = device_rank * shard_text + jnp.arange(shard_text) < text_len[0]
    local_keys = jnp.concatenate([local_video[1, 0], own_text[1]], axis=0)
    local_values = jnp.concatenate([local_video[2, 0], own_text[2]], axis=0)
    local_valid = jnp.concatenate([jnp.ones((positions,), bool), own_valid])
    query_scores = (
        jnp.einsum("thd,khd->thk", text_queries, local_keys, preferred_element_type=f32)
        * score_scale
    )
    query_scores = jnp.where(local_valid, query_scores, masked_score)
    local_max = query_scores.max(-1)
    global_max = lax.pmax(local_max, "frame")
    query_exp = jnp.exp(query_scores - global_max[..., None])
    query_totals = query_exp.sum(-1)
    query_sums = jnp.einsum(
        "thk,khd->thd", query_exp.astype(bf16), local_values, preferred_element_type=f32
    )
    query_sums = lax.psum_scatter(query_sums, "frame", scatter_dimension=0, tiled=True)
    query_totals = lax.psum_scatter(query_totals, "frame", scatter_dimension=0, tiled=True)
    text_out = (query_sums / query_totals[..., None]).astype(bf16).reshape(shard_text, head_width)
    return (video_out, text_out)


def dot_nt(a, b):
    return lax.dot_general(a, b, (((1,), (1,)), ((), ())), preferred_element_type=f32)


def dot_nn(a, b):
    return lax.dot_general(a, b, (((1,), (0,)), ((), ())), preferred_element_type=f32)


def attend(q, keys, values, ok, scale):
    s = jnp.where(ok, dot_nt(q, keys), masked_score)
    top = s.max(-1, keepdims=True)
    w = jnp.exp2((s - top) * scale).astype(bf16)
    hd = values.shape[1]
    both = dot_nn(w, jnp.concatenate([values, jnp.ones_like(values)], axis=1))
    return top, both[:, hd:], both[:, :hd]


def remote(src, dst, send_sem, recv_sem, peer):
    return pltpu.make_async_remote_copy(
        src_ref=src,
        dst_ref=dst,
        send_sem=send_sem,
        recv_sem=recv_sem,
        device_id={"frame": peer},
        device_id_type=pl.DeviceIdType.MESH,
    )


names = (
    "pair_video",
    "pair_text",
    "q_far",
    "q_first",
    "q_second",
    "kv_far",
    "kv_first",
    "kv_second",
    "kv_row",
    "kv_core",
    "part",
    "part_far",
    "attended",
    "temporal0",
    "temporal1",
    "temporal2",
)
sem_at = {name: i for i, name in enumerate(names)}


def kernel(
    heads,
    kind_hbm,
    len_hbm,
    video_hbm,
    text_hbm,
    result,
    text_out,
    kind_ref,
    len_ref,
    video_ref,
    text_ref,
    pair_video,
    pair_text,
    q_all,
    kv_all,
    t_send,
    t_recv,
    o_send,
    o_recv,
    p_send,
    p_recv,
    p_out,
    p_far,
    in_sem,
    send_sem,
    recv_sem,
):
    n = 16
    half = heads // 2
    third = half // 2
    positions, hd = video_ref.shape[2:]
    shard = text_ref.shape[2]
    width = heads * hd
    owned = positions // 8
    scale = hd ** (-0.5) * log2_e
    me = lax.axis_index("frame")
    core = lax.rem(me, 2)
    y = lax.rem(me // 2, 2)
    z = me // 4
    u = lax.rem(me // 2, 4)
    zh = me // 8
    chip = me // 2
    far = lax.rem(me + 8, n)
    z_near = z + 1 - 2 * lax.rem(z, 2)
    z_far = lax.rem(z + 2, 4)
    near = z_near * 4 + y * 2 + core
    across = me + 2 - 4 * y
    partner = me + 1 - 2 * core

    barrier = pltpu.get_barrier_semaphore()

    def greet(k, c):
        pl.semaphore_signal(
            barrier,
            inc=1,
            device_id={"frame": lax.rem(me + k, n)},
            device_id_type=pl.DeviceIdType.MESH,
        )
        return c

    pltpu.make_async_copy(kind_hbm, kind_ref, in_sem.at[0]).start()
    pltpu.make_async_copy(len_hbm, len_ref, in_sem.at[1]).start()
    for src, dst, i in ((text_hbm, text_ref, 2), (video_hbm, video_ref, 3)):
        for h in range(heads):
            hs = slice(h * hd, (h + 1) * hd)
            pltpu.make_async_copy(src.at[:, :, hs], dst.at[:, h], in_sem.at[i]).start()
    lax.fori_loop(1, n, greet, 0)
    for i, ref in enumerate((kind_ref, len_ref, text_ref)):
        pltpu.make_async_copy(ref, ref, in_sem.at[i]).wait()

    seen = [jnp.int32(0), jnp.int32(0)]
    places = []
    for h in range(heads):
        kind = kind_ref[h]
        places.append(jnp.where(kind == 0, seen[0], half + seen[1]))
        seen[0] = seen[0] + jnp.where(kind == 0, 1, 0)
        seen[1] = seen[1] + jnp.where(kind == 0, 0, 1)

    def head_of(i):
        first = i % half
        head = jnp.int32(first)
        for h in range(first + 1, first + half + 1):
            head = jnp.where(places[h] == i, h, head)
        return head

    head_in = [head_of(i) for i in range(heads)]

    for i in range(half):
        for t in range(2):
            kv_all[core, y, z, t, :, i * hd : (i + 1) * hd] = text_ref[t + 1, head_in[i]]
    for h in range(heads):
        q_all[u, zh, :, h * hd : (h + 1) * hd] = text_ref[0, h]

    def start(name, src, dst, to):
        i = sem_at[name]
        remote(src, dst, send_sem.at[i], recv_sem.at[i], to).start()

    def keep(name, src, dst):
        pltpu.make_async_copy(src, dst, recv_sem.at[sem_at[name]]).start()

    def landed(name, like):
        i = sem_at[name]
        remote(like, like, send_sem.at[i], recv_sem.at[i], partner).wait_recv()

    def sent(name, like):
        i = sem_at[name]
        remote(like, like, send_sem.at[i], recv_sem.at[i], partner).wait_send()

    def to_peers(name, block_of):
        def go(k, c):
            v = lax.rem(u + k, 4)
            src, dst = block_of(v)
            start(name, src, dst, zh * 8 + v * 2 + core)
            return c

        lax.fori_loop(1, 4, go, 0)

    pl.semaphore_wait(barrier, n - 1)

    mine = q_all.at[u, zh]
    start("q_far", mine, mine, far)
    to_peers("q_first", lambda v: (mine, mine))
    kv_mine = kv_all.at[core, y, z]
    start("kv_far", kv_mine, kv_mine, far)
    start("kv_first", kv_mine, kv_mine, near)
    start("pair_video", video_hbm.at[1:3], pair_video, partner)
    start("pair_text", text_hbm.at[1:3], pair_text, partner)

    pltpu.make_async_copy(video_ref, video_ref, in_sem.at[3]).wait()

    def pack(i):
        for k in range(2):
            head = head_in[half + third * k + i]
            for t in range(3):
                block = video_ref[t, head].reshape(8, owned, hd)
                t_send[i, :, k, t] = block

    def start_t(i):
        name = f"temporal{i}"
        keep(name, t_send.at[i, chip, core], t_recv.at[i, me])

        def go(k, c):
            to = lax.rem(me + k, n)
            start(name, t_send.at[i, to // 2, lax.rem(to, 2)], t_recv.at[i, me], to)
            return c

        lax.fori_loop(1, n, go, 0)

    pack(0)
    start_t(0)
    pack(1)
    pack(2)

    landed("q_far", mine)
    relayed = q_all.at[u, 1 - zh]
    to_peers("q_second", lambda v: (relayed, relayed))
    landed("kv_far", kv_mine)
    kv_relayed = kv_all.at[core, y, z_far]
    start("kv_second", kv_relayed, kv_relayed, near)
    start_t(1)

    landed("q_first", q_all.at[0:3, 0])
    landed("q_second", q_all.at[0:3, 0])
    landed("pair_video", pair_video)
    landed("pair_text", pair_text)

    length = len_ref[0]
    key = lax.broadcasted_iota(jnp.int32, (1, 2 * positions + 2 * shard), 1)
    offset = key - 2 * positions
    token = jnp.where(offset < shard, me * shard + offset, partner * shard + offset - shard)
    key_ok = (offset < 0) | (token < length)
    rows = 8 * shard
    lane = lax.broadcasted_iota(jnp.int32, (rows, 128), 1)
    tops = jnp.zeros((rows, 128), f32)
    sums = jnp.ones((rows, 128), f32)
    for h in range(heads):
        hs = slice(h * hd, (h + 1) * hd)
        q = q_all[:, :, :, hs].reshape(rows, hd)
        keys, values = (
            jnp.concatenate(
                [video_ref[t + 1, h], pair_video[t, :, hs], text_ref[t + 1, h], pair_text[t, :, hs]],
                axis=0,
            )
            for t in range(2)
        )
        top, total, summed = attend(q, keys, values, key_ok, scale)
        p_send[:, :, :, hs] = (summed / total).astype(bf16).reshape(4, 2, shard, hd)
        tops = jnp.where(lane == h, top, tops)
        sums = jnp.where(lane == h, total, sums)

    def coded(logs):
        at = lax.broadcasted_iota(jnp.int32, logs.shape, 1)
        high = logs.astype(bf16).astype(f32)
        middle = (logs - high).astype(bf16).astype(f32)
        low = logs - high - middle
        return jnp.where(
            at < 16, high, jnp.where(at < 32, pltpu.roll(middle, 16, 1), pltpu.roll(low, 32, 1))
        ).astype(bf16)

    def decoded(code):
        code = code.astype(f32)
        return code + pltpu.roll(code, 112, 1) + pltpu.roll(code, 96, 1)

    p_send[:, :, :, width:] = coded(tops * scale + jnp.log(sums) * log2_e).reshape(4, 2, shard, 128)
    keep("part", p_send.at[u], p_recv.at[u])
    to_peers("part", lambda v: (p_send.at[v], p_recv.at[u]))
    start_t(2)

    landed("kv_first", kv_mine)
    landed("kv_second", kv_mine)
    column = kv_all.at[core, y]
    start("kv_row", column, column, across)

    row_at = lax.rem(lax.broadcasted_iota(jnp.int32, (n * owned, n * owned), 0), owned)
    col_at = lax.rem(lax.broadcasted_iota(jnp.int32, (n * owned, n * owned), 1), owned)
    same = row_at == col_at

    def temporal(i):
        landed(f"temporal{i}", t_recv.at[i])
        q, k_, v = (t_recv[i, :, t].reshape(n * owned, hd) for t in range(3))
        _, total, summed = attend(q, k_, v, same, scale)
        o_send[i] = (summed / total).astype(bf16).reshape(n, owned, hd)
        dst = o_recv.at[third * core + i, chip]
        keep("attended", o_send.at[i, me], dst)

        def go(k, c):
            to = lax.rem(me + k, n)
            start("attended", o_send.at[i, to], dst, to)
            return c

        lax.fori_loop(1, n, go, 0)

    temporal(0)
    temporal(1)

    def combine(parts):
        logs = [decoded(p[:, width:]) for p in parts]
        best = functools.reduce(jnp.maximum, logs)
        weights = [jnp.exp2(jnp.minimum(log - best, 0.0)) for log in logs]
        total = functools.reduce(jnp.add, weights)
        weights = [w / total for w in weights]
        blocks = []
        for h in range(heads):
            hs = slice(h * hd, (h + 1) * hd)
            terms = [w[:, h : h + 1] * p[:, hs].astype(f32) for w, p in zip(weights, parts)]
            blocks.append(functools.reduce(jnp.add, terms).astype(bf16))
        return blocks, best + jnp.log(total) * log2_e

    landed("part", p_recv)
    blocks, logs = combine([p_recv[v, 1 - zh] for v in range(4)])
    for h in range(heads):
        p_out[:, h * hd : (h + 1) * hd] = blocks[h]
    p_out[:, width:] = coded(logs)
    start("part_far", p_out, p_far, far)

    landed("kv_row", column)
    ours = kv_all.at[core]
    start("kv_core", ours, ours, partner)

    temporal(2)

    landed("kv_core", ours)
    at = lax.broadcasted_iota(jnp.int32, (1, positions + n * shard), 1) - positions
    block = jnp.maximum(at, 0) // shard
    source = lax.rem(block, 4) * 4 + lax.rem(block // 4, 2) * 2 + block // 8
    joint_ok = (at < 0) | (source * shard + lax.rem(jnp.maximum(at, 0), shard) < length)
    for i in range(half):
        hs = slice(i * hd, (i + 1) * hd)
        keys, values = (
            jnp.concatenate(
                [video_ref[t + 1, head_in[i]], kv_all[:, :, :, t, :, hs].reshape(n * shard, hd)],
                axis=0,
            )
            for t in range(2)
        )
        _, total, summed = attend(video_ref[0, head_in[i]], keys, values, joint_ok, scale)
        result[i] = (summed / total).astype(bf16)

    landed("part_far", p_out)
    blocks, _ = combine([p_recv[v, zh] for v in range(4)] + [p_far[...]])
    for h in range(heads):
        text_out[:, h * hd : (h + 1) * hd] = blocks[h]

    landed("attended", o_recv)
    for i in range(half):
        result[half + i] = o_recv[i].reshape(positions, hd)

    sent("pair_video", pair_video)
    sent("pair_text", pair_text)
    sent("q_far", mine)
    sent("q_first", q_all.at[0:3, 0])
    sent("q_second", q_all.at[0:3, 0])
    sent("kv_far", kv_mine)
    sent("kv_first", kv_mine)
    sent("kv_second", kv_mine)
    sent("kv_row", column)
    sent("kv_core", ours)
    sent("part", p_send.at[0:3])
    sent("part_far", p_out)
    for i in range(3):
        sent(f"temporal{i}", t_recv.at[i, 0 : n - 1])
    sent("attended", o_send.at[:, 0 : n - 1])


def place_kernel(heads, kind_ref, blocks, text, video_out, text_out, sem):
    half = heads // 2
    hd = blocks.shape[2]
    copies = [pltpu.make_async_copy(text, text_out, sem)]
    seen = [jnp.int32(0), jnp.int32(0)]
    for h in range(heads):
        kind = kind_ref[h]
        place = jnp.where(kind == 0, jnp.minimum(seen[0], half - 1), half + jnp.minimum(seen[1], half - 1))
        seen[0] = seen[0] + jnp.where(kind == 0, 1, 0)
        seen[1] = seen[1] + jnp.where(kind == 0, 0, 1)
        out = video_out.at[:, h * hd : (h + 1) * hd]
        copies.append(pltpu.make_async_copy(blocks.at[place], out, sem))
    for copy in copies:
        copy.start()
    for copy in copies:
        copy.wait()


def fused_body(video_qkv, text_qkv, head_kind, text_len):
    heads = head_kind.shape[0]
    _, _, positions, width = video_qkv.shape
    shard = text_qkv.shape[1]
    n, half, hd = 16, heads // 2, width // heads
    owned, narrow, coded = positions // 8, half * hd, width + 128
    vmem = pl.BlockSpec(memory_space=pltpu.VMEM)
    hbm = pl.BlockSpec(memory_space=pltpu.HBM)
    dma = pltpu.SemaphoreType.DMA
    kind, video, words = (
        pltpu.with_memory_space_constraint(a, pltpu.HBM)
        for a in (head_kind, video_qkv.reshape(3, positions, width), text_qkv)
    )
    inputs = (kind, text_len, video, words)
    blocks, text = pl.pallas_call(
        functools.partial(kernel, heads),
        out_shape=(
            pltpu.VMEM((heads, positions, hd), bf16),
            pltpu.VMEM((shard, width), bf16),
        ),
        in_specs=[hbm] * 4,
        out_specs=(vmem, vmem),
        scratch_shapes=[
            pltpu.SMEM((heads,), jnp.int32),
            pltpu.SMEM((1,), jnp.int32),
            pltpu.VMEM((3, heads, positions, hd), bf16),
            pltpu.VMEM((3, heads, shard, hd), bf16),
            pltpu.VMEM((2, positions, width), bf16),
            pltpu.VMEM((2, shard, width), bf16),
            pltpu.VMEM((4, 2, shard, width), bf16),
            pltpu.VMEM((2, 2, 4, 2, shard, narrow), bf16),
            pltpu.VMEM((3, 8, 2, 3, owned, hd), bf16),
            pltpu.VMEM((3, n, 3, owned, hd), bf16),
            pltpu.VMEM((3, n, owned, hd), bf16),
            pltpu.VMEM((half, 8, owned, hd), bf16),
            pltpu.VMEM((4, 2, shard, coded), bf16),
            pltpu.VMEM((4, 2, shard, coded), bf16),
            pltpu.VMEM((shard, coded), bf16),
            pltpu.VMEM((shard, coded), bf16),
            dma((4,)),
            dma((len(names),)),
            dma((len(names),)),
        ],
        compiler_params=pltpu.CompilerParams(
            collective_id=0, has_side_effects=True, vmem_limit_bytes=24 << 20
        ),
    )(*inputs)
    video_out, text_out = pl.pallas_call(
        functools.partial(place_kernel, heads),
        out_shape=(
            jax.ShapeDtypeStruct((positions, width), bf16),
            jax.ShapeDtypeStruct((shard, width), bf16),
        ),
        in_specs=[pl.BlockSpec(memory_space=pltpu.SMEM), vmem, vmem],
        out_specs=(hbm, hbm),
        scratch_shapes=[dma(())],
        compiler_params=pltpu.CompilerParams(vmem_limit_bytes=8 << 20),
    )(head_kind, blocks, text)
    return video_out.reshape(1, positions, width), text_out


def body(n, video_qkv, text_qkv, head_kind, text_len):
    heads = head_kind.shape[0]
    positions, width = video_qkv.shape[2:]
    shard = text_qkv.shape[1]
    whole_tiles = (
        video_qkv.shape[1] == 1
        and n == 16
        and heads == 12
        and shard % 16 == 0
        and positions % 128 == 0
        and width == heads * 128
    )
    if whole_tiles:
        return fused_body(video_qkv, text_qkv, head_kind, text_len)
    return plain_body(video_qkv, text_qkv, head_kind, text_len)


def solution(mesh):
    in_specs = (
        P(None, ("groups", "frame"), None, None),
        P(None, ("groups", "frame"), None),
        P("groups"),
        P("groups"),
    )
    out_specs = (P(("groups", "frame"), None, None), P(("groups", "frame"), None))
    return jax.shard_map(
        functools.partial(body, mesh.shape["frame"]),
        mesh=mesh,
        in_specs=in_specs,
        out_specs=out_specs,
        check_vma=False,
    )
```

```python
import functools

import jax
import jax.numpy as jnp
import numpy as np
from jax import lax
from jax.experimental import pallas as pl
from jax.experimental.pallas import tpu as pltpu
from jax.sharding import PartitionSpec as P

masked_score = -1e30
log2_e = float(np.log2(np.e))
f32 = jnp.float32
bf16 = jnp.bfloat16


def pick(one_hot, array, dims):
    return jnp.einsum(dims, one_hot, array, preferred_element_type=f32).astype(bf16)


def plain_body(video_qkv, text_qkv, head_kind, text_len):
    head_count = head_kind.shape[0]
    head_width = video_qkv.shape[-1]
    head_dim = head_width // head_count
    positions = video_qkv.shape[2]
    shard_text = text_qkv.shape[1]
    half = head_count // 2
    score_scale = head_dim ** (-0.5)
    device_rank = lax.axis_index("frame")
    local_video = video_qkv.reshape(3, 1, positions, head_count, head_dim)
    gathered = lax.all_gather(text_qkv, "frame", axis=1, tiled=True)
    text_total = gathered.shape[1]
    all_text = gathered.reshape(3, text_total, head_count, head_dim)
    text_valid = jnp.arange(text_total) < text_len[0]
    head_at = jnp.arange(head_count)
    earlier = head_at[None, :] < head_at[:, None]
    same_kind = head_kind[None, :] == head_kind[:, None]
    rank = jnp.sum(jnp.where(earlier & same_kind, 1, 0), axis=1)
    place = rank + half * head_kind
    slots = (place[None, :] == head_at[:, None]).astype(bf16)
    spatial, temporal = slots[:half], slots[half:]
    own_frame = pick(spatial, local_video[:, 0], "ih,tphd->tpid")
    text_spatial = pick(spatial, all_text[1:], "ih,tphd->tpid")
    joint_keys = jnp.concatenate([own_frame[1], text_spatial[0]], axis=0)
    joint_values = jnp.concatenate([own_frame[2], text_spatial[1]], axis=0)
    joint_valid = jnp.concatenate([jnp.ones((positions,), bool), text_valid])
    spatial_scores = (
        jnp.einsum("phd,khd->hpk", own_frame[0], joint_keys, preferred_element_type=f32)
        * score_scale
    )
    spatial_scores = jnp.where(joint_valid, spatial_scores, masked_score)
    row_max = spatial_scores.max(-1, keepdims=True)
    spatial_exp = jnp.exp(spatial_scores - row_max)
    totals = spatial_exp.sum(-1)
    summed = jnp.einsum(
        "hpk,khd->phd", spatial_exp.astype(bf16), joint_values, preferred_element_type=f32
    )
    spatial_result = (summed / totals.T[..., None]).astype(bf16)
    selected = pick(temporal, local_video, "ih,tfphd->tfpid")
    block = lax.all_to_all(selected, "frame", split_axis=2, concat_axis=1, tiled=True)
    scores = (
        jnp.einsum("fphd,gphd->phfg", block[0], block[1], preferred_element_type=f32) * score_scale
    )
    block_max = scores.max(-1, keepdims=True)
    exps = jnp.exp(scores - block_max)
    block_totals = exps.sum(-1)
    block_sum = jnp.einsum(
        "phfg,gphd->fphd", exps.astype(bf16), block[2], preferred_element_type=f32
    )
    result = (block_sum / jnp.transpose(block_totals, (2, 0, 1))[..., None]).astype(bf16)
    temporal_result = lax.all_to_all(result, "frame", split_axis=0, concat_axis=1, tiled=True)[0]
    joined = jnp.concatenate([spatial_result, temporal_result], axis=1)
    video_out = pick(slots, joined, "ih,pid->phd").reshape(1, positions, head_width)
    text_queries = all_text[0]
    own_text = text_qkv.reshape(3, shard_text, head_count, head_dim)
    own_valid = device_rank * shard_text + jnp.arange(shard_text) < text_len[0]
    local_keys = jnp.concatenate([local_video[1, 0], own_text[1]], axis=0)
    local_values = jnp.concatenate([local_video[2, 0], own_text[2]], axis=0)
    local_valid = jnp.concatenate([jnp.ones((positions,), bool), own_valid])
    query_scores = (
        jnp.einsum("thd,khd->thk", text_queries, local_keys, preferred_element_type=f32)
        * score_scale
    )
    query_scores = jnp.where(local_valid, query_scores, masked_score)
    local_max = query_scores.max(-1)
    global_max = lax.pmax(local_max, "frame")
    query_exp = jnp.exp(query_scores - global_max[..., None])
    query_totals = query_exp.sum(-1)
    query_sums = jnp.einsum(
        "thk,khd->thd", query_exp.astype(bf16), local_values, preferred_element_type=f32
    )
    query_sums = lax.psum_scatter(query_sums, "frame", scatter_dimension=0, tiled=True)
    query_totals = lax.psum_scatter(query_totals, "frame", scatter_dimension=0, tiled=True)
    text_out = (query_sums / query_totals[..., None]).astype(bf16).reshape(shard_text, head_width)
    return (video_out, text_out)


def dot_nt(a, b):
    return lax.dot_general(a, b, (((1,), (1,)), ((), ())), preferred_element_type=f32)


def dot_nn(a, b):
    return lax.dot_general(a, b, (((1,), (0,)), ((), ())), preferred_element_type=f32)


def attend(q, keys, values, ok, scale):
    s = jnp.where(ok, dot_nt(q, keys), masked_score)
    top = s.max(-1, keepdims=True)
    w = jnp.exp2((s - top) * scale).astype(bf16)
    hd = values.shape[1]
    both = dot_nn(w, jnp.concatenate([values, jnp.ones_like(values)], axis=1))
    return top, both[:, hd:], both[:, :hd]


def remote(src, dst, send_sem, recv_sem, peer):
    return pltpu.make_async_remote_copy(
        src_ref=src,
        dst_ref=dst,
        send_sem=send_sem,
        recv_sem=recv_sem,
        device_id={"frame": peer},
        device_id_type=pl.DeviceIdType.MESH,
    )


names = (
    "pair_video",
    "pair_text",
    "q_far",
    "q_first",
    "q_second",
    "q_row",
    "kv_far",
    "kv_first",
    "kv_second",
    "kv_row",
    "kv_core",
    "kv_own",
    "part",
    "part_far",
    "attended",
    "temporal0",
    "temporal1",
    "temporal2",
)
sem_at = {name: i for i, name in enumerate(names)}


def kernel(
    heads,
    kind_hbm,
    len_hbm,
    video_hbm,
    text_hbm,
    video_out,
    text_out,
    kind_ref,
    len_ref,
    head_ref,
    place_ref,
    video_ref,
    text_ref,
    pair_video,
    pair_text,
    q_all,
    kv_all,
    t_send,
    t_recv,
    o_send,
    o_recv,
    p_send,
    p_recv,
    p_out,
    p_far,
    result,
    in_sem,
    send_sem,
    recv_sem,
):
    n = 16
    half = heads // 2
    third = half // 2
    positions, hd = video_ref.shape[2:]
    shard = text_ref.shape[2]
    width = heads * hd
    owned = positions // 8
    scale = hd ** (-0.5) * log2_e
    me = lax.axis_index("frame")
    core = lax.rem(me, 2)
    y = lax.rem(me // 2, 2)
    z = me // 4
    u = lax.rem(me // 2, 4)
    zh = me // 8
    chip = me // 2
    far = lax.rem(me + 8, n)
    z_near = z + 1 - 2 * lax.rem(z, 2)
    z_far = lax.rem(z + 2, 4)
    near = z_near * 4 + y * 2 + core
    across = me + 2 - 4 * y
    partner = me + 1 - 2 * core

    barrier = pltpu.get_barrier_semaphore()

    def greet(k, c):
        pl.semaphore_signal(
            barrier,
            inc=1,
            device_id={"frame": lax.rem(me + k, n)},
            device_id_type=pl.DeviceIdType.MESH,
        )
        return c

    pltpu.make_async_copy(kind_hbm, kind_ref, in_sem.at[0]).start()
    pltpu.make_async_copy(len_hbm, len_ref, in_sem.at[1]).start()
    for src, dst, i in ((text_hbm, text_ref, 2), (video_hbm, video_ref, 3)):
        for h in range(heads):
            hs = slice(h * hd, (h + 1) * hd)
            pltpu.make_async_copy(src.at[:, :, hs], dst.at[:, h], in_sem.at[i]).start()
    lax.fori_loop(1, n, greet, 0)
    def prepare():
        for i, ref in enumerate((kind_ref, len_ref, text_ref)):
            pltpu.make_async_copy(ref, ref, in_sem.at[i]).wait()
        seen = [jnp.int32(0), jnp.int32(0)]
        places = []
        for h in range(heads):
            kind = kind_ref[h]
            places.append(jnp.where(kind == 0, seen[0], half + seen[1]))
            place_ref[h] = places[h]
            seen[0] = seen[0] + jnp.where(kind == 0, 1, 0)
            seen[1] = seen[1] + jnp.where(kind == 0, 0, 1)
        head_in = []
        for i in range(heads):
            first = i % half
            head = jnp.int32(first)
            for h in range(first + 1, first + half + 1):
                head = jnp.where(places[h] == i, h, head)
            head_ref[i] = head
            head_in.append(head)
        for i in range(half):
            for t in range(2):
                kv_all[core, y, z, t, :, i * hd : (i + 1) * hd] = text_ref[t + 1, head_in[i]]
        for h in range(heads):
            q_all[u, zh, :, h * hd : (h + 1) * hd] = text_ref[0, h]
        pltpu.make_async_copy(video_ref, video_ref, in_sem.at[3]).wait()
        for i in range(3):
            for k in range(2):
                for t in range(3):
                    block = video_ref[t, head_in[half + third * k + i]].reshape(8, owned, hd)
                    t_send[i, :, k, t] = block

    def start(name, src, dst, to):
        i = sem_at[name]
        remote(src, dst, send_sem.at[i], recv_sem.at[i], to).start()

    def keep(name, src, dst):
        pltpu.make_async_copy(src, dst, recv_sem.at[sem_at[name]]).start()

    def landed(name, like):
        i = sem_at[name]
        remote(like, like, send_sem.at[i], recv_sem.at[i], partner).wait_recv()

    def sent(name, like):
        i = sem_at[name]
        remote(like, like, send_sem.at[i], recv_sem.at[i], partner).wait_send()

    def to_peers(name, block_of):
        def go(k, c):
            v = lax.rem(u + k, 4)
            src, dst = block_of(v)
            start(name, src, dst, zh * 8 + v * 2 + core)
            return c

        lax.fori_loop(1, 4, go, 0)

    early = z < 2
    pl.when(early)(prepare)

    pl.semaphore_wait(barrier, n - 1)

    mine = q_all.at[u, zh]
    words = text_hbm.at[0]
    start("q_far", words, mine, far)
    start("q_first", words, mine, near)
    start("q_row", words, mine, across)
    start("pair_video", video_hbm.at[1:3], pair_video, partner)
    start("pair_text", text_hbm.at[1:3], pair_text, partner)

    pl.when(jnp.logical_not(early))(prepare)

    kv_mine = kv_all.at[core, y, z]
    start("kv_far", kv_mine, kv_mine, far)
    start("kv_first", kv_mine, kv_mine, near)
    start("kv_row", kv_mine, kv_mine, across)

    def start_t(i):
        name = f"temporal{i}"
        keep(name, t_send.at[i, chip, core], t_recv.at[i, me])

        def go(k, c):
            to = lax.rem(me + k, n)
            start(name, t_send.at[i, to // 2, lax.rem(to, 2)], t_recv.at[i, me], to)
            return c

        lax.fori_loop(1, n, go, 0)

    start_t(0)

    landed("q_first", mine)
    q_near = q_all.at[lax.rem(u + 2, 4), zh]
    start("q_row", q_near, q_near, across)
    landed("q_far", mine)
    relayed = q_all.at[u, 1 - zh]
    to_peers("q_second", lambda v: (relayed, relayed))
    landed("kv_far", kv_mine)
    kv_relayed = kv_all.at[core, y, z_far]
    start("kv_second", kv_relayed, kv_relayed, near)
    start("kv_row", kv_relayed, kv_relayed, across)
    start_t(1)

    landed("q_row", q_all.at[0:2, 0])
    landed("q_second", q_all.at[0:3, 0])
    landed("pair_video", pair_video)
    landed("pair_text", pair_text)

    length = len_ref[0]
    key = lax.broadcasted_iota(jnp.int32, (1, 2 * positions + 2 * shard), 1)
    offset = key - 2 * positions
    token = jnp.where(offset < shard, me * shard + offset, partner * shard + offset - shard)
    key_ok = (offset < 0) | (token < length)
    rows = 8 * shard
    lane = lax.broadcasted_iota(jnp.int32, (rows, 128), 1)
    tops = jnp.zeros((rows, 128), f32)
    sums = jnp.ones((rows, 128), f32)
    for h in range(heads):
        hs = slice(h * hd, (h + 1) * hd)
        q = q_all[:, :, :, hs].reshape(rows, hd)
        keys, values = (
            jnp.concatenate(
                [video_ref[t + 1, h], pair_video[t, :, hs], text_ref[t + 1, h], pair_text[t, :, hs]],
                axis=0,
            )
            for t in range(2)
        )
        top, total, summed = attend(q, keys, values, key_ok, scale)
        p_send[:, :, :, hs] = (summed / total).astype(bf16).reshape(4, 2, shard, hd)
        tops = jnp.where(lane == h, top, tops)
        sums = jnp.where(lane == h, total, sums)

    def coded(logs):
        at = lax.broadcasted_iota(jnp.int32, logs.shape, 1)
        high = logs.astype(bf16).astype(f32)
        middle = (logs - high).astype(bf16).astype(f32)
        low = logs - high - middle
        return jnp.where(
            at < 16, high, jnp.where(at < 32, pltpu.roll(middle, 16, 1), pltpu.roll(low, 32, 1))
        ).astype(bf16)

    def decoded(code):
        code = code.astype(f32)
        return code + pltpu.roll(code, 112, 1) + pltpu.roll(code, 96, 1)

    p_send[:, :, :, width:] = coded(tops * scale + jnp.log(sums) * log2_e).reshape(4, 2, shard, 128)
    keep("part", p_send.at[u], p_recv.at[u])
    to_peers("part", lambda v: (p_send.at[v], p_recv.at[u]))
    start_t(2)

    landed("kv_first", kv_mine)
    landed("kv_second", kv_mine)
    for slot in (z_near, lax.rem(z_near + 2, 4)):
        block = kv_all.at[core, y, slot]
        start("kv_row", block, block, across)
    column = kv_all.at[core, y]
    start("kv_own", column, column, partner)

    row_at = lax.rem(lax.broadcasted_iota(jnp.int32, (n * owned, n * owned), 0), owned)
    col_at = lax.rem(lax.broadcasted_iota(jnp.int32, (n * owned, n * owned), 1), owned)
    same = row_at == col_at

    def temporal(i):
        landed(f"temporal{i}", t_recv.at[i])
        q, k_, v = (t_recv[i, :, t].reshape(n * owned, hd) for t in range(3))
        _, total, summed = attend(q, k_, v, same, scale)
        o_send[i] = (summed / total).astype(bf16).reshape(n, owned, hd)
        dst = o_recv.at[third * core + i, chip]
        keep("attended", o_send.at[i, me], dst)

        def go(k, c):
            to = lax.rem(me + k, n)
            start("attended", o_send.at[i, to], dst, to)
            return c

        lax.fori_loop(1, n, go, 0)

    temporal(0)
    temporal(1)

    def combine(parts):
        logs = [decoded(p[:, width:]) for p in parts]
        best = functools.reduce(jnp.maximum, logs)
        weights = [jnp.exp2(jnp.minimum(log - best, 0.0)) for log in logs]
        total = functools.reduce(jnp.add, weights)
        weights = [w / total for w in weights]
        blocks = []
        for h in range(heads):
            hs = slice(h * hd, (h + 1) * hd)
            terms = [w[:, h : h + 1] * p[:, hs].astype(f32) for w, p in zip(weights, parts)]
            blocks.append(functools.reduce(jnp.add, terms).astype(bf16))
        return blocks, best + jnp.log(total) * log2_e

    landed("part", p_recv)
    blocks, logs = combine([p_recv[v, 1 - zh] for v in range(4)])
    for h in range(heads):
        p_out[:, h * hd : (h + 1) * hd] = blocks[h]
    p_out[:, width:] = coded(logs)
    start("part_far", p_out, p_far, far)

    landed("kv_row", column)
    ours = kv_all.at[core, 1 - y]
    start("kv_core", ours, ours, partner)
    landed("kv_own", column)

    landed("kv_core", ours)
    at = lax.broadcasted_iota(jnp.int32, (1, positions + n * shard), 1) - positions
    block = jnp.maximum(at, 0) // shard
    source = lax.rem(block, 4) * 4 + lax.rem(block // 4, 2) * 2 + block // 8
    joint_ok = (at < 0) | (source * shard + lax.rem(jnp.maximum(at, 0), shard) < length)
    for i in range(half):
        hs = slice(i * hd, (i + 1) * hd)
        keys, values = (
            jnp.concatenate(
                [video_ref[t + 1, head_ref[i]], kv_all[:, :, :, t, :, hs].reshape(n * shard, hd)],
                axis=0,
            )
            for t in range(2)
        )
        _, total, summed = attend(video_ref[0, head_ref[i]], keys, values, joint_ok, scale)
        result[i] = (summed / total).astype(bf16)

    temporal(2)

    landed("part_far", p_out)
    blocks, _ = combine([p_recv[v, zh] for v in range(4)] + [p_far[...]])
    for h in range(heads):
        text_out[:, h * hd : (h + 1) * hd] = blocks[h]

    landed("attended", o_recv)
    for h in range(heads):
        spatial = result[jnp.minimum(place_ref[h], half - 1)]
        temporal_block = o_recv[jnp.maximum(place_ref[h] - half, 0)].reshape(positions, hd)
        video_out[:, h * hd : (h + 1) * hd] = jnp.where(place_ref[h] < half, spatial, temporal_block)

    sent("pair_video", pair_video)
    sent("pair_text", pair_text)
    sent("q_far", mine)
    sent("q_first", mine)
    sent("q_row", q_all.at[0:2, 0])
    sent("q_second", q_all.at[0:3, 0])
    sent("kv_far", kv_mine)
    sent("kv_first", kv_mine)
    sent("kv_second", kv_mine)
    sent("kv_row", column)
    sent("kv_core", ours)
    sent("kv_own", column)
    sent("part", p_send.at[0:3])
    sent("part_far", p_out)
    for i in range(3):
        sent(f"temporal{i}", t_recv.at[i, 0 : n - 1])
    sent("attended", o_send.at[:, 0 : n - 1])


def hand_over(video, text, video_out, text_out, sem):
    copies = [
        pltpu.make_async_copy(video, video_out, sem.at[0]),
        pltpu.make_async_copy(text, text_out, sem.at[1]),
    ]
    for copy in copies:
        copy.start()
    for copy in copies:
        copy.wait()


def fused_body(video_qkv, text_qkv, head_kind, text_len):
    heads = head_kind.shape[0]
    _, _, positions, width = video_qkv.shape
    shard = text_qkv.shape[1]
    n, half, hd = 16, heads // 2, width // heads
    owned, narrow, coded = positions // 8, half * hd, width + 128
    vmem = pl.BlockSpec(memory_space=pltpu.VMEM)
    hbm = pl.BlockSpec(memory_space=pltpu.HBM)
    dma = pltpu.SemaphoreType.DMA
    kind, video, words = (
        pltpu.with_memory_space_constraint(a, pltpu.HBM)
        for a in (head_kind, video_qkv.reshape(3, positions, width), text_qkv)
    )
    held = pl.pallas_call(
        functools.partial(kernel, heads),
        out_shape=(
            pltpu.VMEM((positions, width), bf16),
            pltpu.VMEM((shard, width), bf16),
        ),
        in_specs=[hbm] * 4,
        out_specs=(vmem, vmem),
        scratch_shapes=[
            pltpu.SMEM((heads,), jnp.int32),
            pltpu.SMEM((1,), jnp.int32),
            pltpu.SMEM((heads,), jnp.int32),
            pltpu.SMEM((heads,), jnp.int32),
            pltpu.VMEM((3, heads, positions, hd), bf16),
            pltpu.VMEM((3, heads, shard, hd), bf16),
            pltpu.VMEM((2, positions, width), bf16),
            pltpu.VMEM((2, shard, width), bf16),
            pltpu.VMEM((4, 2, shard, width), bf16),
            pltpu.VMEM((2, 2, 4, 2, shard, narrow), bf16),
            pltpu.VMEM((3, 8, 2, 3, owned, hd), bf16),
            pltpu.VMEM((3, n, 3, owned, hd), bf16),
            pltpu.VMEM((3, n, owned, hd), bf16),
            pltpu.VMEM((half, 8, owned, hd), bf16),
            pltpu.VMEM((4, 2, shard, coded), bf16),
            pltpu.VMEM((4, 2, shard, coded), bf16),
            pltpu.VMEM((shard, coded), bf16),
            pltpu.VMEM((shard, coded), bf16),
            pltpu.VMEM((half, positions, hd), bf16),
            dma((4,)),
            dma((len(names),)),
            dma((len(names),)),
        ],
        compiler_params=pltpu.CompilerParams(
            collective_id=0, has_side_effects=True, vmem_limit_bytes=24 << 20
        ),
    )(kind, text_len, video, words)
    video_out, text_out = pl.pallas_call(
        hand_over,
        out_shape=(
            jax.ShapeDtypeStruct((positions, width), bf16),
            jax.ShapeDtypeStruct((shard, width), bf16),
        ),
        in_specs=[vmem, vmem],
        out_specs=(hbm, hbm),
        scratch_shapes=[dma((2,))],
        compiler_params=pltpu.CompilerParams(vmem_limit_bytes=8 << 20),
    )(*held)
    return video_out.reshape(1, positions, width), text_out


def body(n, video_qkv, text_qkv, head_kind, text_len):
    heads = head_kind.shape[0]
    positions, width = video_qkv.shape[2:]
    shard = text_qkv.shape[1]
    whole_tiles = (
        video_qkv.shape[1] == 1
        and n == 16
        and heads == 12
        and shard % 16 == 0
        and positions % 128 == 0
        and width == heads * 128
    )
    if whole_tiles:
        return fused_body(video_qkv, text_qkv, head_kind, text_len)
    return plain_body(video_qkv, text_qkv, head_kind, text_len)


def solution(mesh):
    in_specs = (
        P(None, ("groups", "frame"), None, None),
        P(None, ("groups", "frame"), None),
        P("groups"),
        P("groups"),
    )
    out_specs = (P(("groups", "frame"), None, None), P(("groups", "frame"), None))
    return jax.shard_map(
        functools.partial(body, mesh.shape["frame"]),
        mesh=mesh,
        in_specs=in_specs,
        out_specs=out_specs,
        check_vma=False,
    )
```

```python
import functools

import jax
import jax.numpy as jnp
import numpy as np
from jax import lax
from jax.experimental import pallas as pl
from jax.experimental.pallas import tpu as pltpu
from jax.sharding import PartitionSpec as P

masked_score = -1e30
log2_e = float(np.log2(np.e))
f32 = jnp.float32
bf16 = jnp.bfloat16


def pick(one_hot, array, dims):
    return jnp.einsum(dims, one_hot, array, preferred_element_type=f32).astype(bf16)


def plain_body(video_qkv, text_qkv, head_kind, text_len):
    head_count = head_kind.shape[0]
    head_width = video_qkv.shape[-1]
    head_dim = head_width // head_count
    positions = video_qkv.shape[2]
    shard_text = text_qkv.shape[1]
    half = head_count // 2
    score_scale = head_dim ** (-0.5)
    device_rank = lax.axis_index("frame")
    local_video = video_qkv.reshape(3, 1, positions, head_count, head_dim)
    gathered = lax.all_gather(text_qkv, "frame", axis=1, tiled=True)
    text_total = gathered.shape[1]
    all_text = gathered.reshape(3, text_total, head_count, head_dim)
    text_valid = jnp.arange(text_total) < text_len[0]
    head_at = jnp.arange(head_count)
    earlier = head_at[None, :] < head_at[:, None]
    same_kind = head_kind[None, :] == head_kind[:, None]
    rank = jnp.sum(jnp.where(earlier & same_kind, 1, 0), axis=1)
    place = rank + half * head_kind
    slots = (place[None, :] == head_at[:, None]).astype(bf16)
    spatial, temporal = slots[:half], slots[half:]
    own_frame = pick(spatial, local_video[:, 0], "ih,tphd->tpid")
    text_spatial = pick(spatial, all_text[1:], "ih,tphd->tpid")
    joint_keys = jnp.concatenate([own_frame[1], text_spatial[0]], axis=0)
    joint_values = jnp.concatenate([own_frame[2], text_spatial[1]], axis=0)
    joint_valid = jnp.concatenate([jnp.ones((positions,), bool), text_valid])
    spatial_scores = (
        jnp.einsum("phd,khd->hpk", own_frame[0], joint_keys, preferred_element_type=f32)
        * score_scale
    )
    spatial_scores = jnp.where(joint_valid, spatial_scores, masked_score)
    row_max = spatial_scores.max(-1, keepdims=True)
    spatial_exp = jnp.exp(spatial_scores - row_max)
    totals = spatial_exp.sum(-1)
    summed = jnp.einsum(
        "hpk,khd->phd", spatial_exp.astype(bf16), joint_values, preferred_element_type=f32
    )
    spatial_result = (summed / totals.T[..., None]).astype(bf16)
    selected = pick(temporal, local_video, "ih,tfphd->tfpid")
    block = lax.all_to_all(selected, "frame", split_axis=2, concat_axis=1, tiled=True)
    scores = (
        jnp.einsum("fphd,gphd->phfg", block[0], block[1], preferred_element_type=f32) * score_scale
    )
    block_max = scores.max(-1, keepdims=True)
    exps = jnp.exp(scores - block_max)
    block_totals = exps.sum(-1)
    block_sum = jnp.einsum(
        "phfg,gphd->fphd", exps.astype(bf16), block[2], preferred_element_type=f32
    )
    result = (block_sum / jnp.transpose(block_totals, (2, 0, 1))[..., None]).astype(bf16)
    temporal_result = lax.all_to_all(result, "frame", split_axis=0, concat_axis=1, tiled=True)[0]
    joined = jnp.concatenate([spatial_result, temporal_result], axis=1)
    video_out = pick(slots, joined, "ih,pid->phd").reshape(1, positions, head_width)
    text_queries = all_text[0]
    own_text = text_qkv.reshape(3, shard_text, head_count, head_dim)
    own_valid = device_rank * shard_text + jnp.arange(shard_text) < text_len[0]
    local_keys = jnp.concatenate([local_video[1, 0], own_text[1]], axis=0)
    local_values = jnp.concatenate([local_video[2, 0], own_text[2]], axis=0)
    local_valid = jnp.concatenate([jnp.ones((positions,), bool), own_valid])
    query_scores = (
        jnp.einsum("thd,khd->thk", text_queries, local_keys, preferred_element_type=f32)
        * score_scale
    )
    query_scores = jnp.where(local_valid, query_scores, masked_score)
    local_max = query_scores.max(-1)
    global_max = lax.pmax(local_max, "frame")
    query_exp = jnp.exp(query_scores - global_max[..., None])
    query_totals = query_exp.sum(-1)
    query_sums = jnp.einsum(
        "thk,khd->thd", query_exp.astype(bf16), local_values, preferred_element_type=f32
    )
    query_sums = lax.psum_scatter(query_sums, "frame", scatter_dimension=0, tiled=True)
    query_totals = lax.psum_scatter(query_totals, "frame", scatter_dimension=0, tiled=True)
    text_out = (query_sums / query_totals[..., None]).astype(bf16).reshape(shard_text, head_width)
    return (video_out, text_out)


def dot_nt(a, b):
    return lax.dot_general(a, b, (((1,), (1,)), ((), ())), preferred_element_type=f32)


def dot_nn(a, b):
    return lax.dot_general(a, b, (((1,), (0,)), ((), ())), preferred_element_type=f32)


def attend(q, keys, values, ok, scale):
    s = jnp.where(ok, dot_nt(q, keys), masked_score)
    top = s.max(-1, keepdims=True)
    w = jnp.exp2((s - top) * scale).astype(bf16)
    hd = values.shape[1]
    both = dot_nn(w, jnp.concatenate([values, jnp.ones_like(values)], axis=1))
    return top, both[:, hd:], both[:, :hd]


def remote(src, dst, send_sem, recv_sem, peer):
    return pltpu.make_async_remote_copy(
        src_ref=src,
        dst_ref=dst,
        send_sem=send_sem,
        recv_sem=recv_sem,
        device_id={"frame": peer},
        device_id_type=pl.DeviceIdType.MESH,
    )


names = (
    "pair_video",
    "pair_text",
    "q_far",
    "q_first",
    "q_second",
    "q_row",
    "kv_far",
    "kv_first",
    "kv_second",
    "kv_row",
    "kv_core",
    "kv_own",
    "part",
    "part_own",
    "part_far",
    "attended",
    "temporal0",
    "temporal1",
    "temporal2",
)
sem_at = {name: i for i, name in enumerate(names)}


def kernel(
    heads,
    kind_hbm,
    len_hbm,
    video_hbm,
    text_hbm,
    video_out,
    text_out,
    kind_ref,
    len_ref,
    head_ref,
    place_ref,
    video_ref,
    text_ref,
    pair_video,
    pair_text,
    q_all,
    kv_all,
    t_send,
    t_recv,
    o_send,
    o_recv,
    p_send,
    p_recv,
    p_out,
    p_far,
    result,
    in_sem,
    send_sem,
    recv_sem,
):
    n = 16
    half = heads // 2
    third = half // 2
    positions, hd = video_ref.shape[2:]
    shard = text_ref.shape[2]
    width = heads * hd
    owned = positions // 8
    scale = hd ** (-0.5) * log2_e
    me = lax.axis_index("frame")
    core = lax.rem(me, 2)
    y = lax.rem(me // 2, 2)
    z = me // 4
    u = lax.rem(me // 2, 4)
    zh = me // 8
    chip = me // 2
    far = lax.rem(me + 8, n)
    z_near = z + 1 - 2 * lax.rem(z, 2)
    z_far = lax.rem(z + 2, 4)
    near = z_near * 4 + y * 2 + core
    across = me + 2 - 4 * y
    partner = me + 1 - 2 * core

    barrier = pltpu.get_barrier_semaphore()

    def greet(k, c):
        pl.semaphore_signal(
            barrier,
            inc=1,
            device_id={"frame": lax.rem(me + k, n)},
            device_id_type=pl.DeviceIdType.MESH,
        )
        return c

    lax.fori_loop(1, n, greet, 0)
    pltpu.make_async_copy(kind_hbm, kind_ref, in_sem.at[0]).start()
    pltpu.make_async_copy(len_hbm, len_ref, in_sem.at[1]).start()
    for src, dst, i in ((text_hbm, text_ref, 2), (video_hbm, video_ref, 3)):
        for h in range(heads):
            hs = slice(h * hd, (h + 1) * hd)
            pltpu.make_async_copy(src.at[:, :, hs], dst.at[:, h], in_sem.at[i]).start()
    def prepare():
        for i, ref in enumerate((kind_ref, len_ref, text_ref)):
            pltpu.make_async_copy(ref, ref, in_sem.at[i]).wait()
        seen = [jnp.int32(0), jnp.int32(0)]
        places = []
        for h in range(heads):
            kind = kind_ref[h]
            places.append(jnp.where(kind == 0, seen[0], half + seen[1]))
            place_ref[h] = places[h]
            seen[0] = seen[0] + jnp.where(kind == 0, 1, 0)
            seen[1] = seen[1] + jnp.where(kind == 0, 0, 1)
        head_in = []
        for i in range(heads):
            first = i % half
            head = jnp.int32(first)
            for h in range(first + 1, first + half + 1):
                head = jnp.where(places[h] == i, h, head)
            head_ref[i] = head
            head_in.append(head)
        for i in range(half):
            for t in range(2):
                kv_all[core, y, z, t, :, i * hd : (i + 1) * hd] = text_ref[t + 1, head_in[i]]
        for h in range(heads):
            q_all[u, zh, :, h * hd : (h + 1) * hd] = text_ref[0, h]
        pltpu.make_async_copy(video_ref, video_ref, in_sem.at[3]).wait()
        for i in range(3):
            for k in range(2):
                for t in range(3):
                    block = video_ref[t, head_in[half + third * k + i]].reshape(8, owned, hd)
                    t_send[i, :, k, t] = block

    def start(name, src, dst, to):
        i = sem_at[name]
        remote(src, dst, send_sem.at[i], recv_sem.at[i], to).start()

    def keep(name, src, dst):
        pltpu.make_async_copy(src, dst, recv_sem.at[sem_at[name]]).start()

    def landed(name, like):
        i = sem_at[name]
        remote(like, like, send_sem.at[i], recv_sem.at[i], partner).wait_recv()

    def sent(name, like):
        i = sem_at[name]
        remote(like, like, send_sem.at[i], recv_sem.at[i], partner).wait_send()

    def to_peers(name, block_of):
        def go(k, c):
            v = lax.rem(u + k, 4)
            src, dst = block_of(v)
            start(name, src, dst, zh * 8 + v * 2 + core)
            return c

        lax.fori_loop(1, 4, go, 0)

    early = z < 2
    pl.when(early)(prepare)

    pl.semaphore_wait(barrier, n - 1)

    mine = q_all.at[u, zh]
    words = text_hbm.at[0]
    start("q_far", words, mine, far)
    start("q_first", words, mine, near)
    start("q_row", words, mine, across)
    start("pair_video", video_hbm.at[1:3], pair_video, partner)
    start("pair_text", text_hbm.at[1:3], pair_text, partner)

    pl.when(jnp.logical_not(early))(prepare)

    kv_mine = kv_all.at[core, y, z]
    start("kv_far", kv_mine, kv_mine, far)
    start("kv_first", kv_mine, kv_mine, near)
    start("kv_row", kv_mine, kv_mine, across)

    def start_t(i):
        name = f"temporal{i}"
        keep(name, t_send.at[i, chip, core], t_recv.at[i, me])

        def go(k, c):
            to = lax.rem(me + lax.rem(k + 10, 15) + 1, n)
            start(name, t_send.at[i, to // 2, lax.rem(to, 2)], t_recv.at[i, me], to)
            return c

        lax.fori_loop(1, n, go, 0)

    start_t(0)

    landed("q_first", mine)
    q_near = q_all.at[lax.rem(u + 2, 4), zh]
    start("q_row", q_near, q_near, across)
    landed("q_far", mine)
    relayed = q_all.at[u, 1 - zh]
    to_peers("q_second", lambda v: (relayed, relayed))
    landed("kv_far", kv_mine)
    kv_relayed = kv_all.at[core, y, z_far]
    start("kv_second", kv_relayed, kv_relayed, near)
    start("kv_row", kv_relayed, kv_relayed, across)
    start_t(1)

    landed("q_row", q_all.at[0:2, 0])
    landed("pair_video", pair_video)
    landed("pair_text", pair_text)

    length = len_ref[0]
    key = lax.broadcasted_iota(jnp.int32, (1, 2 * positions + 2 * shard), 1)
    offset = key - 2 * positions
    token = jnp.where(offset < shard, me * shard + offset, partner * shard + offset - shard)
    key_ok = (offset < 0) | (token < length)
    rows = 4 * shard
    lane = lax.broadcasted_iota(jnp.int32, (rows, 128), 1)

    def coded(logs):
        at = lax.broadcasted_iota(jnp.int32, logs.shape, 1)
        high = logs.astype(bf16).astype(f32)
        middle = (logs - high).astype(bf16).astype(f32)
        low = logs - high - middle
        return jnp.where(
            at < 16, high, jnp.where(at < 32, pltpu.roll(middle, 16, 1), pltpu.roll(low, 32, 1))
        ).astype(bf16)

    def decoded(code):
        code = code.astype(f32)
        return code + pltpu.roll(code, 112, 1) + pltpu.roll(code, 96, 1)

    def partial(side):
        tops = jnp.zeros((rows, 128), f32)
        sums = jnp.ones((rows, 128), f32)
        for h in range(heads):
            hs = slice(h * hd, (h + 1) * hd)
            q = q_all[:, side, :, hs].reshape(rows, hd)
            keys, values = (
                jnp.concatenate(
                    [video_ref[t + 1, h], pair_video[t, :, hs], text_ref[t + 1, h], pair_text[t, :, hs]],
                    axis=0,
                )
                for t in range(2)
            )
            top, total, summed = attend(q, keys, values, key_ok, scale)
            p_send[:, side, :, hs] = (summed / total).astype(bf16).reshape(4, shard, hd)
            tops = jnp.where(lane == h, top, tops)
            sums = jnp.where(lane == h, total, sums)
        logs = coded(tops * scale + jnp.log(sums) * log2_e)
        p_send[:, side, :, width:] = logs.reshape(4, shard, 128)

    def give(name, side):
        keep(name, p_send.at[u, side], p_recv.at[u, side])
        to_peers(name, lambda v: (p_send.at[v, side], p_recv.at[u, side]))

    partial(zh)

    landed("q_second", q_all.at[0:3, 0])
    partial(1 - zh)
    give("part", 1 - zh)
    start_t(2)

    landed("kv_first", kv_mine)
    landed("kv_second", kv_mine)
    for slot in (z_near, lax.rem(z_near + 2, 4)):
        block = kv_all.at[core, y, slot]
        start("kv_row", block, block, across)
    column = kv_all.at[core, y]
    start("kv_own", column, column, partner)

    row_at = lax.rem(lax.broadcasted_iota(jnp.int32, (n * owned, n * owned), 0), owned)
    col_at = lax.rem(lax.broadcasted_iota(jnp.int32, (n * owned, n * owned), 1), owned)
    same = row_at == col_at

    def temporal(i):
        landed(f"temporal{i}", t_recv.at[i])
        q, k_, v = (t_recv[i, :, t].reshape(n * owned, hd) for t in range(3))
        _, total, summed = attend(q, k_, v, same, scale)
        o_send[i] = (summed / total).astype(bf16).reshape(n, owned, hd)
        dst = o_recv.at[third * core + i, chip]
        keep("attended", o_send.at[i, me], dst)

        def go(k, c):
            to = lax.rem(me + k, n)
            start("attended", o_send.at[i, to], dst, to)
            return c

        lax.fori_loop(1, n, go, 0)

    temporal(0)
    temporal(1)
    give("part_own", zh)

    def combine(parts):
        logs = [decoded(p[:, width:]) for p in parts]
        best = functools.reduce(jnp.maximum, logs)
        weights = [jnp.exp2(jnp.minimum(log - best, 0.0)) for log in logs]
        total = functools.reduce(jnp.add, weights)
        weights = [w / total for w in weights]
        blocks = []
        for h in range(heads):
            hs = slice(h * hd, (h + 1) * hd)
            terms = [w[:, h : h + 1] * p[:, hs].astype(f32) for w, p in zip(weights, parts)]
            blocks.append(functools.reduce(jnp.add, terms).astype(bf16))
        return blocks, best + jnp.log(total) * log2_e

    landed("part", p_recv.at[:, 0])
    blocks, logs = combine([p_recv[v, 1 - zh] for v in range(4)])
    for h in range(heads):
        p_out[:, h * hd : (h + 1) * hd] = blocks[h]
    p_out[:, width:] = coded(logs)
    start("part_far", p_out, p_far, far)

    temporal(2)

    landed("kv_row", column)
    ours = kv_all.at[core, 1 - y]
    start("kv_core", ours, ours, partner)
    landed("kv_own", column)

    landed("kv_core", ours)
    at = lax.broadcasted_iota(jnp.int32, (1, positions + n * shard), 1) - positions
    block = jnp.maximum(at, 0) // shard
    source = lax.rem(block, 4) * 4 + lax.rem(block // 4, 2) * 2 + block // 8
    joint_ok = (at < 0) | (source * shard + lax.rem(jnp.maximum(at, 0), shard) < length)
    for i in range(half):
        hs = slice(i * hd, (i + 1) * hd)
        keys, values = (
            jnp.concatenate(
                [video_ref[t + 1, head_ref[i]], kv_all[:, :, :, t, :, hs].reshape(n * shard, hd)],
                axis=0,
            )
            for t in range(2)
        )
        _, total, summed = attend(video_ref[0, head_ref[i]], keys, values, joint_ok, scale)
        result[i] = (summed / total).astype(bf16)

    landed("part_own", p_recv.at[:, 0])
    landed("part_far", p_out)
    blocks, _ = combine([p_recv[v, zh] for v in range(4)] + [p_far[...]])
    for h in range(heads):
        text_out[:, h * hd : (h + 1) * hd] = blocks[h]

    landed("attended", o_recv)
    for h in range(heads):
        spatial = result[jnp.minimum(place_ref[h], half - 1)]
        temporal_block = o_recv[jnp.maximum(place_ref[h] - half, 0)].reshape(positions, hd)
        video_out[:, h * hd : (h + 1) * hd] = jnp.where(place_ref[h] < half, spatial, temporal_block)

    sent("pair_video", pair_video)
    sent("pair_text", pair_text)
    sent("q_far", mine)
    sent("q_first", mine)
    sent("q_row", q_all.at[0:2, 0])
    sent("q_second", q_all.at[0:3, 0])
    sent("kv_far", kv_mine)
    sent("kv_first", kv_mine)
    sent("kv_second", kv_mine)
    sent("kv_row", column)
    sent("kv_core", ours)
    sent("kv_own", column)
    sent("part", p_send.at[0:3, 0])
    sent("part_own", p_send.at[0:3, 0])
    sent("part_far", p_out)
    for i in range(3):
        sent(f"temporal{i}", t_recv.at[i, 0 : n - 1])
    sent("attended", o_send.at[:, 0 : n - 1])


def hand_over(video, text, video_out, text_out, sem):
    copies = [
        pltpu.make_async_copy(video, video_out, sem.at[0]),
        pltpu.make_async_copy(text, text_out, sem.at[1]),
    ]
    for copy in copies:
        copy.start()
    for copy in copies:
        copy.wait()


def fused_body(video_qkv, text_qkv, head_kind, text_len):
    heads = head_kind.shape[0]
    _, _, positions, width = video_qkv.shape
    shard = text_qkv.shape[1]
    n, half, hd = 16, heads // 2, width // heads
    owned, narrow, coded = positions // 8, half * hd, width + 128
    vmem = pl.BlockSpec(memory_space=pltpu.VMEM)
    hbm = pl.BlockSpec(memory_space=pltpu.HBM)
    dma = pltpu.SemaphoreType.DMA
    kind, video, words = (
        pltpu.with_memory_space_constraint(a, pltpu.HBM)
        for a in (head_kind, video_qkv.reshape(3, positions, width), text_qkv)
    )
    held = pl.pallas_call(
        functools.partial(kernel, heads),
        out_shape=(
            pltpu.VMEM((positions, width), bf16),
            pltpu.VMEM((shard, width), bf16),
        ),
        in_specs=[hbm] * 4,
        out_specs=(vmem, vmem),
        scratch_shapes=[
            pltpu.SMEM((heads,), jnp.int32),
            pltpu.SMEM((1,), jnp.int32),
            pltpu.SMEM((heads,), jnp.int32),
            pltpu.SMEM((heads,), jnp.int32),
            pltpu.VMEM((3, heads, positions, hd), bf16),
            pltpu.VMEM((3, heads, shard, hd), bf16),
            pltpu.VMEM((2, positions, width), bf16),
            pltpu.VMEM((2, shard, width), bf16),
            pltpu.VMEM((4, 2, shard, width), bf16),
            pltpu.VMEM((2, 2, 4, 2, shard, narrow), bf16),
            pltpu.VMEM((3, 8, 2, 3, owned, hd), bf16),
            pltpu.VMEM((3, n, 3, owned, hd), bf16),
            pltpu.VMEM((3, n, owned, hd), bf16),
            pltpu.VMEM((half, 8, owned, hd), bf16),
            pltpu.VMEM((4, 2, shard, coded), bf16),
            pltpu.VMEM((4, 2, shard, coded), bf16),
            pltpu.VMEM((shard, coded), bf16),
            pltpu.VMEM((shard, coded), bf16),
            pltpu.VMEM((half, positions, hd), bf16),
            dma((4,)),
            dma((len(names),)),
            dma((len(names),)),
        ],
        compiler_params=pltpu.CompilerParams(
            collective_id=0, has_side_effects=True, vmem_limit_bytes=24 << 20
        ),
    )(kind, text_len, video, words)
    video_out, text_out = pl.pallas_call(
        hand_over,
        out_shape=(
            jax.ShapeDtypeStruct((positions, width), bf16),
            jax.ShapeDtypeStruct((shard, width), bf16),
        ),
        in_specs=[vmem, vmem],
        out_specs=(hbm, hbm),
        scratch_shapes=[dma((2,))],
        compiler_params=pltpu.CompilerParams(vmem_limit_bytes=8 << 20),
    )(*held)
    return video_out.reshape(1, positions, width), text_out


def body(n, video_qkv, text_qkv, head_kind, text_len):
    heads = head_kind.shape[0]
    positions, width = video_qkv.shape[2:]
    shard = text_qkv.shape[1]
    whole_tiles = (
        video_qkv.shape[1] == 1
        and n == 16
        and heads == 12
        and shard % 16 == 0
        and positions % 128 == 0
        and width == heads * 128
    )
    if whole_tiles:
        return fused_body(video_qkv, text_qkv, head_kind, text_len)
    return plain_body(video_qkv, text_qkv, head_kind, text_len)


def solution(mesh):
    in_specs = (
        P(None, ("groups", "frame"), None, None),
        P(None, ("groups", "frame"), None),
        P("groups"),
        P("groups"),
    )
    out_specs = (P(("groups", "frame"), None, None), P(("groups", "frame"), None))
    return jax.shard_map(
        functools.partial(body, mesh.shape["frame"]),
        mesh=mesh,
        in_specs=in_specs,
        out_specs=out_specs,
        check_vma=False,
    )
```

```python
import functools

import jax
import jax.numpy as jnp
import numpy as np
from jax import lax
from jax.experimental import pallas as pl
from jax.experimental.pallas import tpu as pltpu
from jax.sharding import PartitionSpec as P

masked_score = -1e30
log2_e = float(np.log2(np.e))
f32 = jnp.float32
bf16 = jnp.bfloat16


def pick(one_hot, array, dims):
    return jnp.einsum(dims, one_hot, array, preferred_element_type=f32).astype(bf16)


def plain_body(video_qkv, text_qkv, head_kind, text_len):
    head_count = head_kind.shape[0]
    head_width = video_qkv.shape[-1]
    head_dim = head_width // head_count
    positions = video_qkv.shape[2]
    shard_text = text_qkv.shape[1]
    half = head_count // 2
    score_scale = head_dim ** (-0.5)
    device_rank = lax.axis_index("frame")
    local_video = video_qkv.reshape(3, 1, positions, head_count, head_dim)
    gathered = lax.all_gather(text_qkv, "frame", axis=1, tiled=True)
    text_total = gathered.shape[1]
    all_text = gathered.reshape(3, text_total, head_count, head_dim)
    text_valid = jnp.arange(text_total) < text_len[0]
    head_at = jnp.arange(head_count)
    earlier = head_at[None, :] < head_at[:, None]
    same_kind = head_kind[None, :] == head_kind[:, None]
    rank = jnp.sum(jnp.where(earlier & same_kind, 1, 0), axis=1)
    place = rank + half * head_kind
    slots = (place[None, :] == head_at[:, None]).astype(bf16)
    spatial, temporal = slots[:half], slots[half:]
    own_frame = pick(spatial, local_video[:, 0], "ih,tphd->tpid")
    text_spatial = pick(spatial, all_text[1:], "ih,tphd->tpid")
    joint_keys = jnp.concatenate([own_frame[1], text_spatial[0]], axis=0)
    joint_values = jnp.concatenate([own_frame[2], text_spatial[1]], axis=0)
    joint_valid = jnp.concatenate([jnp.ones((positions,), bool), text_valid])
    spatial_scores = (
        jnp.einsum("phd,khd->hpk", own_frame[0], joint_keys, preferred_element_type=f32)
        * score_scale
    )
    spatial_scores = jnp.where(joint_valid, spatial_scores, masked_score)
    row_max = spatial_scores.max(-1, keepdims=True)
    spatial_exp = jnp.exp(spatial_scores - row_max)
    totals = spatial_exp.sum(-1)
    summed = jnp.einsum(
        "hpk,khd->phd", spatial_exp.astype(bf16), joint_values, preferred_element_type=f32
    )
    spatial_result = (summed / totals.T[..., None]).astype(bf16)
    selected = pick(temporal, local_video, "ih,tfphd->tfpid")
    block = lax.all_to_all(selected, "frame", split_axis=2, concat_axis=1, tiled=True)
    scores = (
        jnp.einsum("fphd,gphd->phfg", block[0], block[1], preferred_element_type=f32) * score_scale
    )
    block_max = scores.max(-1, keepdims=True)
    exps = jnp.exp(scores - block_max)
    block_totals = exps.sum(-1)
    block_sum = jnp.einsum(
        "phfg,gphd->fphd", exps.astype(bf16), block[2], preferred_element_type=f32
    )
    result = (block_sum / jnp.transpose(block_totals, (2, 0, 1))[..., None]).astype(bf16)
    temporal_result = lax.all_to_all(result, "frame", split_axis=0, concat_axis=1, tiled=True)[0]
    joined = jnp.concatenate([spatial_result, temporal_result], axis=1)
    video_out = pick(slots, joined, "ih,pid->phd").reshape(1, positions, head_width)
    text_queries = all_text[0]
    own_text = text_qkv.reshape(3, shard_text, head_count, head_dim)
    own_valid = device_rank * shard_text + jnp.arange(shard_text) < text_len[0]
    local_keys = jnp.concatenate([local_video[1, 0], own_text[1]], axis=0)
    local_values = jnp.concatenate([local_video[2, 0], own_text[2]], axis=0)
    local_valid = jnp.concatenate([jnp.ones((positions,), bool), own_valid])
    query_scores = (
        jnp.einsum("thd,khd->thk", text_queries, local_keys, preferred_element_type=f32)
        * score_scale
    )
    query_scores = jnp.where(local_valid, query_scores, masked_score)
    local_max = query_scores.max(-1)
    global_max = lax.pmax(local_max, "frame")
    query_exp = jnp.exp(query_scores - global_max[..., None])
    query_totals = query_exp.sum(-1)
    query_sums = jnp.einsum(
        "thk,khd->thd", query_exp.astype(bf16), local_values, preferred_element_type=f32
    )
    query_sums = lax.psum_scatter(query_sums, "frame", scatter_dimension=0, tiled=True)
    query_totals = lax.psum_scatter(query_totals, "frame", scatter_dimension=0, tiled=True)
    text_out = (query_sums / query_totals[..., None]).astype(bf16).reshape(shard_text, head_width)
    return (video_out, text_out)


def dot_nt(a, b):
    return lax.dot_general(a, b, (((1,), (1,)), ((), ())), preferred_element_type=f32)


def dot_nn(a, b):
    return lax.dot_general(a, b, (((1,), (0,)), ((), ())), preferred_element_type=f32)


def attend(q, keys, values, ok, scale):
    s = jnp.where(ok, dot_nt(q, keys), masked_score)
    top = s.max(-1, keepdims=True)
    w = jnp.exp2((s - top) * scale).astype(bf16)
    hd = values.shape[1]
    both = dot_nn(w, jnp.concatenate([values, jnp.ones_like(values)], axis=1))
    return top, both[:, hd:], both[:, :hd]


def remote(src, dst, send_sem, recv_sem, peer):
    return pltpu.make_async_remote_copy(
        src_ref=src,
        dst_ref=dst,
        send_sem=send_sem,
        recv_sem=recv_sem,
        device_id={"frame": peer},
        device_id_type=pl.DeviceIdType.MESH,
    )


names = (
    "pair_video",
    "pair_text",
    "q_far",
    "q_first",
    "q_second",
    "q_row",
    "kv_far",
    "kv_first",
    "kv_second",
    "kv_row",
    "kv_core",
    "kv_own",
    "part",
    "part_own",
    "part_far",
    "attended",
    "temporal0",
    "temporal1",
    "temporal2",
)
sem_at = {name: i for i, name in enumerate(names)}


def kernel(
    heads,
    kind_hbm,
    len_hbm,
    video_hbm,
    text_hbm,
    video_out,
    text_out,
    kind_ref,
    len_ref,
    head_ref,
    place_ref,
    video_ref,
    text_ref,
    pair_video,
    pair_text,
    q_all,
    kv_all,
    t_send,
    t_recv,
    o_send,
    o_recv,
    p_send,
    p_recv,
    p_out,
    p_far,
    result,
    in_sem,
    send_sem,
    recv_sem,
):
    n = 16
    half = heads // 2
    third = half // 2
    positions, hd = video_ref.shape[2:]
    shard = text_ref.shape[2]
    width = heads * hd
    owned = positions // 8
    scale = hd ** (-0.5) * log2_e
    me = lax.axis_index("frame")
    core = lax.rem(me, 2)
    y = lax.rem(me // 2, 2)
    z = me // 4
    u = lax.rem(me // 2, 4)
    zh = me // 8
    chip = me // 2
    far = lax.rem(me + 8, n)
    z_near = z + 1 - 2 * lax.rem(z, 2)
    z_far = lax.rem(z + 2, 4)
    near = z_near * 4 + y * 2 + core
    across = me + 2 - 4 * y
    partner = me + 1 - 2 * core

    barrier = pltpu.get_barrier_semaphore()

    def greet(k, c):
        pl.semaphore_signal(
            barrier,
            inc=1,
            device_id={"frame": lax.rem(me + k, n)},
            device_id_type=pl.DeviceIdType.MESH,
        )
        return c

    lax.fori_loop(1, n, greet, 0)
    pltpu.make_async_copy(kind_hbm, kind_ref, in_sem.at[0]).start()
    pltpu.make_async_copy(len_hbm, len_ref, in_sem.at[1]).start()
    for src, dst, i in ((text_hbm, text_ref, 2), (video_hbm, video_ref, 3)):
        for h in range(heads):
            hs = slice(h * hd, (h + 1) * hd)
            pltpu.make_async_copy(src.at[:, :, hs], dst.at[:, h], in_sem.at[i]).start()
    def prepare():
        for i, ref in enumerate((kind_ref, len_ref, text_ref)):
            pltpu.make_async_copy(ref, ref, in_sem.at[i]).wait()
        seen = [jnp.int32(0), jnp.int32(0)]
        places = []
        for h in range(heads):
            kind = kind_ref[h]
            places.append(jnp.where(kind == 0, seen[0], half + seen[1]))
            place_ref[h] = places[h]
            seen[0] = seen[0] + jnp.where(kind == 0, 1, 0)
            seen[1] = seen[1] + jnp.where(kind == 0, 0, 1)
        head_in = []
        for i in range(heads):
            first = i % half
            head = jnp.int32(first)
            for h in range(first + 1, first + half + 1):
                head = jnp.where(places[h] == i, h, head)
            head_ref[i] = head
            head_in.append(head)
        for i in range(half):
            for t in range(2):
                kv_all[core, y, z, t, :, i * hd : (i + 1) * hd] = text_ref[t + 1, head_in[i]]
        for h in range(heads):
            q_all[u, zh, :, h * hd : (h + 1) * hd] = text_ref[0, h]
        pltpu.make_async_copy(video_ref, video_ref, in_sem.at[3]).wait()
        for i in range(3):
            for k in range(2):
                for t in range(3):
                    block = video_ref[t, head_in[half + third * k + i]].reshape(8, owned, hd)
                    t_send[i, :, k, t] = block

    def start(name, src, dst, to):
        i = sem_at[name]
        remote(src, dst, send_sem.at[i], recv_sem.at[i], to).start()

    def keep(name, src, dst):
        pltpu.make_async_copy(src, dst, recv_sem.at[sem_at[name]]).start()

    def landed(name, like):
        i = sem_at[name]
        remote(like, like, send_sem.at[i], recv_sem.at[i], partner).wait_recv()

    def sent(name, like):
        i = sem_at[name]
        remote(like, like, send_sem.at[i], recv_sem.at[i], partner).wait_send()

    def to_peers(name, block_of):
        def go(k, c):
            v = lax.rem(u + k, 4)
            src, dst = block_of(v)
            start(name, src, dst, zh * 8 + v * 2 + core)
            return c

        lax.fori_loop(1, 4, go, 0)

    early = z < 2
    pl.when(early)(prepare)

    pl.semaphore_wait(barrier, n - 1)

    mine = q_all.at[u, zh]
    words = text_hbm.at[0]
    start("q_far", words, mine, far)
    start("q_first", words, mine, near)
    start("q_row", words, mine, across)
    start("pair_video", video_hbm.at[1:3], pair_video, partner)
    start("pair_text", text_hbm.at[1:3], pair_text, partner)

    pl.when(jnp.logical_not(early))(prepare)

    kv_mine = kv_all.at[core, y, z]
    start("kv_far", kv_mine, kv_mine, far)
    start("kv_first", kv_mine, kv_mine, near)
    start("kv_row", kv_mine, kv_mine, across)

    def start_t(i):
        name = f"temporal{i}"
        keep(name, t_send.at[i, chip, core], t_recv.at[i, me])

        def go(k, c):
            to = lax.rem(me + lax.rem(k + 10, 15) + 1, n)
            start(name, t_send.at[i, to // 2, lax.rem(to, 2)], t_recv.at[i, me], to)
            return c

        lax.fori_loop(1, n, go, 0)

    start_t(0)

    landed("q_first", mine)
    q_near = q_all.at[lax.rem(u + 2, 4), zh]
    start("q_row", q_near, q_near, across)
    landed("q_far", mine)
    relayed = q_all.at[u, 1 - zh]
    to_peers("q_second", lambda v: (relayed, relayed))
    landed("kv_far", kv_mine)
    kv_relayed = kv_all.at[core, y, z_far]
    start("kv_second", kv_relayed, kv_relayed, near)
    start("kv_row", kv_relayed, kv_relayed, across)
    start_t(1)

    row_at = lax.rem(lax.broadcasted_iota(jnp.int32, (n * owned, n * owned), 0), owned)
    col_at = lax.rem(lax.broadcasted_iota(jnp.int32, (n * owned, n * owned), 1), owned)
    same = row_at == col_at

    def temporal(i):
        landed(f"temporal{i}", t_recv.at[i])
        q, k_, v = (t_recv[i, :, t].reshape(n * owned, hd) for t in range(3))
        _, total, summed = attend(q, k_, v, same, scale)
        o_send[i] = (summed / total).astype(bf16).reshape(n, owned, hd)
        dst = o_recv.at[third * core + i, chip]
        keep("attended", o_send.at[i, me], dst)

        def go(k, c):
            to = lax.rem(me + k, n)
            start("attended", o_send.at[i, to], dst, to)
            return c

        lax.fori_loop(1, n, go, 0)

    landed("q_row", q_all.at[0:2, 0])
    landed("pair_video", pair_video)
    landed("pair_text", pair_text)

    length = len_ref[0]
    key = lax.broadcasted_iota(jnp.int32, (1, 2 * positions + 2 * shard), 1)
    offset = key - 2 * positions
    token = jnp.where(offset < shard, me * shard + offset, partner * shard + offset - shard)
    key_ok = (offset < 0) | (token < length)
    rows = 4 * shard
    lane = lax.broadcasted_iota(jnp.int32, (rows, 128), 1)

    def coded(logs):
        at = lax.broadcasted_iota(jnp.int32, logs.shape, 1)
        high = logs.astype(bf16).astype(f32)
        middle = (logs - high).astype(bf16).astype(f32)
        low = logs - high - middle
        return jnp.where(
            at < 16, high, jnp.where(at < 32, pltpu.roll(middle, 16, 1), pltpu.roll(low, 32, 1))
        ).astype(bf16)

    def decoded(code):
        code = code.astype(f32)
        return code + pltpu.roll(code, 112, 1) + pltpu.roll(code, 96, 1)

    def partial(side):
        tops = jnp.zeros((rows, 128), f32)
        sums = jnp.ones((rows, 128), f32)
        for h in range(heads):
            hs = slice(h * hd, (h + 1) * hd)
            q = q_all[:, side, :, hs].reshape(rows, hd)
            keys, values = (
                jnp.concatenate(
                    [video_ref[t + 1, h], pair_video[t, :, hs], text_ref[t + 1, h], pair_text[t, :, hs]],
                    axis=0,
                )
                for t in range(2)
            )
            top, total, summed = attend(q, keys, values, key_ok, scale)
            p_send[:, side, :, hs] = (summed / total).astype(bf16).reshape(4, shard, hd)
            tops = jnp.where(lane == h, top, tops)
            sums = jnp.where(lane == h, total, sums)
        logs = coded(tops * scale + jnp.log(sums) * log2_e)
        p_send[:, side, :, width:] = logs.reshape(4, shard, 128)

    def give(name, side):
        keep(name, p_send.at[u, side], p_recv.at[u, side])
        to_peers(name, lambda v: (p_send.at[v, side], p_recv.at[u, side]))

    partial(zh)

    landed("q_second", q_all.at[0:3, 0])
    partial(1 - zh)
    give("part", 1 - zh)
    start_t(2)
    temporal(0)

    landed("kv_first", kv_mine)
    landed("kv_second", kv_mine)
    for slot in (z_near, lax.rem(z_near + 2, 4)):
        block = kv_all.at[core, y, slot]
        start("kv_row", block, block, across)
    column = kv_all.at[core, y]
    start("kv_own", column, column, partner)

    temporal(1)
    give("part_own", zh)

    def combine(parts):
        logs = [decoded(p[:, width:]) for p in parts]
        best = functools.reduce(jnp.maximum, logs)
        weights = [jnp.exp2(jnp.minimum(log - best, 0.0)) for log in logs]
        total = functools.reduce(jnp.add, weights)
        weights = [w / total for w in weights]
        blocks = []
        for h in range(heads):
            hs = slice(h * hd, (h + 1) * hd)
            terms = [w[:, h : h + 1] * p[:, hs].astype(f32) for w, p in zip(weights, parts)]
            blocks.append(functools.reduce(jnp.add, terms).astype(bf16))
        return blocks, best + jnp.log(total) * log2_e

    landed("part", p_recv.at[:, 0])
    blocks, logs = combine([p_recv[v, 1 - zh] for v in range(4)])
    for h in range(heads):
        p_out[:, h * hd : (h + 1) * hd] = blocks[h]
    p_out[:, width:] = coded(logs)
    start("part_far", p_out, p_far, far)

    temporal(2)

    landed("kv_row", column)
    ours = kv_all.at[core, 1 - y]
    start("kv_core", ours, ours, partner)
    landed("kv_own", column)

    landed("kv_core", ours)
    at = lax.broadcasted_iota(jnp.int32, (1, positions + n * shard), 1) - positions
    block = jnp.maximum(at, 0) // shard
    source = lax.rem(block, 4) * 4 + lax.rem(block // 4, 2) * 2 + block // 8
    joint_ok = (at < 0) | (source * shard + lax.rem(jnp.maximum(at, 0), shard) < length)
    for i in range(half):
        hs = slice(i * hd, (i + 1) * hd)
        keys, values = (
            jnp.concatenate(
                [video_ref[t + 1, head_ref[i]], kv_all[:, :, :, t, :, hs].reshape(n * shard, hd)],
                axis=0,
            )
            for t in range(2)
        )
        _, total, summed = attend(video_ref[0, head_ref[i]], keys, values, joint_ok, scale)
        result[i] = (summed / total).astype(bf16)

    landed("part_own", p_recv.at[:, 0])
    landed("part_far", p_out)
    blocks, _ = combine([p_recv[v, zh] for v in range(4)] + [p_far[...]])
    for h in range(heads):
        text_out[:, h * hd : (h + 1) * hd] = blocks[h]

    landed("attended", o_recv)
    for h in range(heads):
        spatial = result[jnp.minimum(place_ref[h], half - 1)]
        temporal_block = o_recv[jnp.maximum(place_ref[h] - half, 0)].reshape(positions, hd)
        video_out[:, h * hd : (h + 1) * hd] = jnp.where(place_ref[h] < half, spatial, temporal_block)

    sent("pair_video", pair_video)
    sent("pair_text", pair_text)
    sent("q_far", mine)
    sent("q_first", mine)
    sent("q_row", q_all.at[0:2, 0])
    sent("q_second", q_all.at[0:3, 0])
    sent("kv_far", kv_mine)
    sent("kv_first", kv_mine)
    sent("kv_second", kv_mine)
    sent("kv_row", column)
    sent("kv_core", ours)
    sent("kv_own", column)
    sent("part", p_send.at[0:3, 0])
    sent("part_own", p_send.at[0:3, 0])
    sent("part_far", p_out)
    for i in range(3):
        sent(f"temporal{i}", t_recv.at[i, 0 : n - 1])
    sent("attended", o_send.at[:, 0 : n - 1])


def hand_over(video, text, video_out, text_out, sem):
    copies = [
        pltpu.make_async_copy(video, video_out, sem.at[0]),
        pltpu.make_async_copy(text, text_out, sem.at[1]),
    ]
    for copy in copies:
        copy.start()
    for copy in copies:
        copy.wait()


def fused_body(video_qkv, text_qkv, head_kind, text_len):
    heads = head_kind.shape[0]
    _, _, positions, width = video_qkv.shape
    shard = text_qkv.shape[1]
    n, half, hd = 16, heads // 2, width // heads
    owned, narrow, coded = positions // 8, half * hd, width + 128
    vmem = pl.BlockSpec(memory_space=pltpu.VMEM)
    hbm = pl.BlockSpec(memory_space=pltpu.HBM)
    dma = pltpu.SemaphoreType.DMA
    kind, video, words = (
        pltpu.with_memory_space_constraint(a, pltpu.HBM)
        for a in (head_kind, video_qkv.reshape(3, positions, width), text_qkv)
    )
    held = pl.pallas_call(
        functools.partial(kernel, heads),
        out_shape=(
            pltpu.VMEM((positions, width), bf16),
            pltpu.VMEM((shard, width), bf16),
        ),
        in_specs=[hbm] * 4,
        out_specs=(vmem, vmem),
        scratch_shapes=[
            pltpu.SMEM((heads,), jnp.int32),
            pltpu.SMEM((1,), jnp.int32),
            pltpu.SMEM((heads,), jnp.int32),
            pltpu.SMEM((heads,), jnp.int32),
            pltpu.VMEM((3, heads, positions, hd), bf16),
            pltpu.VMEM((3, heads, shard, hd), bf16),
            pltpu.VMEM((2, positions, width), bf16),
            pltpu.VMEM((2, shard, width), bf16),
            pltpu.VMEM((4, 2, shard, width), bf16),
            pltpu.VMEM((2, 2, 4, 2, shard, narrow), bf16),
            pltpu.VMEM((3, 8, 2, 3, owned, hd), bf16),
            pltpu.VMEM((3, n, 3, owned, hd), bf16),
            pltpu.VMEM((3, n, owned, hd), bf16),
            pltpu.VMEM((half, 8, owned, hd), bf16),
            pltpu.VMEM((4, 2, shard, coded), bf16),
            pltpu.VMEM((4, 2, shard, coded), bf16),
            pltpu.VMEM((shard, coded), bf16),
            pltpu.VMEM((shard, coded), bf16),
            pltpu.VMEM((half, positions, hd), bf16),
            dma((4,)),
            dma((len(names),)),
            dma((len(names),)),
        ],
        compiler_params=pltpu.CompilerParams(
            collective_id=0, has_side_effects=True, vmem_limit_bytes=24 << 20
        ),
    )(kind, text_len, video, words)
    video_out, text_out = pl.pallas_call(
        hand_over,
        out_shape=(
            jax.ShapeDtypeStruct((positions, width), bf16),
            jax.ShapeDtypeStruct((shard, width), bf16),
        ),
        in_specs=[vmem, vmem],
        out_specs=(hbm, hbm),
        scratch_shapes=[dma((2,))],
        compiler_params=pltpu.CompilerParams(vmem_limit_bytes=8 << 20),
    )(*held)
    return video_out.reshape(1, positions, width), text_out


def body(n, video_qkv, text_qkv, head_kind, text_len):
    heads = head_kind.shape[0]
    positions, width = video_qkv.shape[2:]
    shard = text_qkv.shape[1]
    whole_tiles = (
        video_qkv.shape[1] == 1
        and n == 16
        and heads == 12
        and shard % 16 == 0
        and positions % 128 == 0
        and width == heads * 128
    )
    if whole_tiles:
        return fused_body(video_qkv, text_qkv, head_kind, text_len)
    return plain_body(video_qkv, text_qkv, head_kind, text_len)


def solution(mesh):
    in_specs = (
        P(None, ("groups", "frame"), None, None),
        P(None, ("groups", "frame"), None),
        P("groups"),
        P("groups"),
    )
    out_specs = (P(("groups", "frame"), None, None), P(("groups", "frame"), None))
    return jax.shard_map(
        functools.partial(body, mesh.shape["frame"]),
        mesh=mesh,
        in_specs=in_specs,
        out_specs=out_specs,
        check_vma=False,
    )
```

```python
import functools

import jax
import jax.numpy as jnp
import numpy as np
from jax import lax
from jax.experimental import pallas as pl
from jax.experimental.pallas import tpu as pltpu
from jax.sharding import PartitionSpec as P

masked_score = -1e30
log2_e = float(np.log2(np.e))
f32 = jnp.float32
bf16 = jnp.bfloat16


def pick(one_hot, array, dims):
    return jnp.einsum(dims, one_hot, array, preferred_element_type=f32).astype(bf16)


def plain_body(video_qkv, text_qkv, head_kind, text_len):
    head_count = head_kind.shape[0]
    head_width = video_qkv.shape[-1]
    head_dim = head_width // head_count
    positions = video_qkv.shape[2]
    shard_text = text_qkv.shape[1]
    half = head_count // 2
    score_scale = head_dim ** (-0.5)
    device_rank = lax.axis_index("frame")
    local_video = video_qkv.reshape(3, 1, positions, head_count, head_dim)
    gathered = lax.all_gather(text_qkv, "frame", axis=1, tiled=True)
    text_total = gathered.shape[1]
    all_text = gathered.reshape(3, text_total, head_count, head_dim)
    text_valid = jnp.arange(text_total) < text_len[0]
    head_at = jnp.arange(head_count)
    earlier = head_at[None, :] < head_at[:, None]
    same_kind = head_kind[None, :] == head_kind[:, None]
    rank = jnp.sum(jnp.where(earlier & same_kind, 1, 0), axis=1)
    place = rank + half * head_kind
    slots = (place[None, :] == head_at[:, None]).astype(bf16)
    spatial, temporal = slots[:half], slots[half:]
    own_frame = pick(spatial, local_video[:, 0], "ih,tphd->tpid")
    text_spatial = pick(spatial, all_text[1:], "ih,tphd->tpid")
    joint_keys = jnp.concatenate([own_frame[1], text_spatial[0]], axis=0)
    joint_values = jnp.concatenate([own_frame[2], text_spatial[1]], axis=0)
    joint_valid = jnp.concatenate([jnp.ones((positions,), bool), text_valid])
    spatial_scores = (
        jnp.einsum("phd,khd->hpk", own_frame[0], joint_keys, preferred_element_type=f32)
        * score_scale
    )
    spatial_scores = jnp.where(joint_valid, spatial_scores, masked_score)
    row_max = spatial_scores.max(-1, keepdims=True)
    spatial_exp = jnp.exp(spatial_scores - row_max)
    totals = spatial_exp.sum(-1)
    summed = jnp.einsum(
        "hpk,khd->phd", spatial_exp.astype(bf16), joint_values, preferred_element_type=f32
    )
    spatial_result = (summed / totals.T[..., None]).astype(bf16)
    selected = pick(temporal, local_video, "ih,tfphd->tfpid")
    block = lax.all_to_all(selected, "frame", split_axis=2, concat_axis=1, tiled=True)
    scores = (
        jnp.einsum("fphd,gphd->phfg", block[0], block[1], preferred_element_type=f32) * score_scale
    )
    block_max = scores.max(-1, keepdims=True)
    exps = jnp.exp(scores - block_max)
    block_totals = exps.sum(-1)
    block_sum = jnp.einsum(
        "phfg,gphd->fphd", exps.astype(bf16), block[2], preferred_element_type=f32
    )
    result = (block_sum / jnp.transpose(block_totals, (2, 0, 1))[..., None]).astype(bf16)
    temporal_result = lax.all_to_all(result, "frame", split_axis=0, concat_axis=1, tiled=True)[0]
    joined = jnp.concatenate([spatial_result, temporal_result], axis=1)
    video_out = pick(slots, joined, "ih,pid->phd").reshape(1, positions, head_width)
    text_queries = all_text[0]
    own_text = text_qkv.reshape(3, shard_text, head_count, head_dim)
    own_valid = device_rank * shard_text + jnp.arange(shard_text) < text_len[0]
    local_keys = jnp.concatenate([local_video[1, 0], own_text[1]], axis=0)
    local_values = jnp.concatenate([local_video[2, 0], own_text[2]], axis=0)
    local_valid = jnp.concatenate([jnp.ones((positions,), bool), own_valid])
    query_scores = (
        jnp.einsum("thd,khd->thk", text_queries, local_keys, preferred_element_type=f32)
        * score_scale
    )
    query_scores = jnp.where(local_valid, query_scores, masked_score)
    local_max = query_scores.max(-1)
    global_max = lax.pmax(local_max, "frame")
    query_exp = jnp.exp(query_scores - global_max[..., None])
    query_totals = query_exp.sum(-1)
    query_sums = jnp.einsum(
        "thk,khd->thd", query_exp.astype(bf16), local_values, preferred_element_type=f32
    )
    query_sums = lax.psum_scatter(query_sums, "frame", scatter_dimension=0, tiled=True)
    query_totals = lax.psum_scatter(query_totals, "frame", scatter_dimension=0, tiled=True)
    text_out = (query_sums / query_totals[..., None]).astype(bf16).reshape(shard_text, head_width)
    return (video_out, text_out)


def dot_nt(a, b):
    return lax.dot_general(a, b, (((1,), (1,)), ((), ())), preferred_element_type=f32)


def dot_nn(a, b):
    return lax.dot_general(a, b, (((1,), (0,)), ((), ())), preferred_element_type=f32)


def attend(q, keys, values, ok, scale):
    s = jnp.where(ok, dot_nt(q, keys), masked_score)
    top = s.max(-1, keepdims=True)
    w = jnp.exp2((s - top) * scale).astype(bf16)
    hd = values.shape[1]
    both = dot_nn(w, jnp.concatenate([values, jnp.ones_like(values)], axis=1))
    return top, both[:, hd:], both[:, :hd]


def remote(src, dst, send_sem, recv_sem, peer):
    return pltpu.make_async_remote_copy(
        src_ref=src,
        dst_ref=dst,
        send_sem=send_sem,
        recv_sem=recv_sem,
        device_id={"frame": peer},
        device_id_type=pl.DeviceIdType.MESH,
    )


names = (
    "pair_video",
    "pair_text",
    "q_far",
    "q_first",
    "q_second",
    "q_row",
    "kv_far",
    "kv_first",
    "kv_second",
    "kv_row",
    "kv_core",
    "kv_own",
    "part",
    "part_row",
    "part_own",
    "part_far",
    "attended",
    "temporal0",
    "temporal1",
    "temporal2",
)
sem_at = {name: i for i, name in enumerate(names)}


def kernel(
    heads,
    kind_hbm,
    len_hbm,
    video_hbm,
    text_hbm,
    video_out,
    text_out,
    kind_ref,
    len_ref,
    head_ref,
    place_ref,
    video_ref,
    text_ref,
    pair_video,
    pair_text,
    q_all,
    kv_all,
    t_send,
    t_recv,
    o_send,
    o_recv,
    p_send,
    p_recv,
    p_mid,
    p_own,
    p_near,
    p_out,
    p_far,
    result,
    in_sem,
    send_sem,
    recv_sem,
):
    n = 16
    half = heads // 2
    third = half // 2
    positions, hd = video_ref.shape[2:]
    shard = text_ref.shape[2]
    width = heads * hd
    owned = positions // 8
    scale = hd ** (-0.5) * log2_e
    me = lax.axis_index("frame")
    core = lax.rem(me, 2)
    y = lax.rem(me // 2, 2)
    z = me // 4
    u = lax.rem(me // 2, 4)
    zh = me // 8
    chip = me // 2
    far = lax.rem(me + 8, n)
    z_near = z + 1 - 2 * lax.rem(z, 2)
    z_far = lax.rem(z + 2, 4)
    near = z_near * 4 + y * 2 + core
    across = me + 2 - 4 * y
    partner = me + 1 - 2 * core

    barrier = pltpu.get_barrier_semaphore()

    def greet(k, c):
        pl.semaphore_signal(
            barrier,
            inc=1,
            device_id={"frame": lax.rem(me + k, n)},
            device_id_type=pl.DeviceIdType.MESH,
        )
        return c

    lax.fori_loop(1, n, greet, 0)
    pltpu.make_async_copy(kind_hbm, kind_ref, in_sem.at[0]).start()
    pltpu.make_async_copy(len_hbm, len_ref, in_sem.at[1]).start()
    for src, dst, i in ((text_hbm, text_ref, 2), (video_hbm, video_ref, 3)):
        for h in range(heads):
            hs = slice(h * hd, (h + 1) * hd)
            pltpu.make_async_copy(src.at[:, :, hs], dst.at[:, h], in_sem.at[i]).start()
    def prepare():
        for i, ref in enumerate((kind_ref, len_ref, text_ref)):
            pltpu.make_async_copy(ref, ref, in_sem.at[i]).wait()
        seen = [jnp.int32(0), jnp.int32(0)]
        places = []
        for h in range(heads):
            kind = kind_ref[h]
            places.append(jnp.where(kind == 0, seen[0], half + seen[1]))
            place_ref[h] = places[h]
            seen[0] = seen[0] + jnp.where(kind == 0, 1, 0)
            seen[1] = seen[1] + jnp.where(kind == 0, 0, 1)
        head_in = []
        for i in range(heads):
            first = i % half
            head = jnp.int32(first)
            for h in range(first + 1, first + half + 1):
                head = jnp.where(places[h] == i, h, head)
            head_ref[i] = head
            head_in.append(head)
        for i in range(half):
            for t in range(2):
                kv_all[core, y, z, t, :, i * hd : (i + 1) * hd] = text_ref[t + 1, head_in[i]]
        for h in range(heads):
            q_all[u, zh, :, h * hd : (h + 1) * hd] = text_ref[0, h]
        pltpu.make_async_copy(video_ref, video_ref, in_sem.at[3]).wait()
        for i in range(3):
            for k in range(2):
                for t in range(3):
                    block = video_ref[t, head_in[half + third * k + i]].reshape(8, owned, hd)
                    t_send[i, :, k, t] = block

    def start(name, src, dst, to):
        i = sem_at[name]
        remote(src, dst, send_sem.at[i], recv_sem.at[i], to).start()

    def keep(name, src, dst):
        pltpu.make_async_copy(src, dst, recv_sem.at[sem_at[name]]).start()

    def landed(name, like):
        i = sem_at[name]
        remote(like, like, send_sem.at[i], recv_sem.at[i], partner).wait_recv()

    def sent(name, like):
        i = sem_at[name]
        remote(like, like, send_sem.at[i], recv_sem.at[i], partner).wait_send()

    def to_peers(name, block_of):
        def go(k, c):
            v = lax.rem(u + k, 4)
            src, dst = block_of(v)
            start(name, src, dst, zh * 8 + v * 2 + core)
            return c

        lax.fori_loop(1, 4, go, 0)

    early = z < 2
    pl.when(early)(prepare)

    pl.semaphore_wait(barrier, n - 1)

    mine = q_all.at[u, zh]
    words = text_hbm.at[0]
    start("q_far", words, mine, far)
    start("q_first", words, mine, near)
    start("q_row", words, mine, across)
    start("pair_video", video_hbm.at[1:3], pair_video, partner)
    start("pair_text", text_hbm.at[1:3], pair_text, partner)

    pl.when(jnp.logical_not(early))(prepare)

    kv_mine = kv_all.at[core, y, z]
    start("kv_far", kv_mine, kv_mine, far)
    start("kv_first", kv_mine, kv_mine, near)
    start("kv_row", kv_mine, kv_mine, across)

    def start_t(i):
        name = f"temporal{i}"
        keep(name, t_send.at[i, chip, core], t_recv.at[i, me])

        def go(k, c):
            to = lax.rem(me + lax.rem(k + 10, 15) + 1, n)
            start(name, t_send.at[i, to // 2, lax.rem(to, 2)], t_recv.at[i, me], to)
            return c

        lax.fori_loop(1, n, go, 0)

    start_t(0)

    landed("q_first", mine)
    q_near = q_all.at[lax.rem(u + 2, 4), zh]
    start("q_row", q_near, q_near, across)
    landed("q_far", mine)
    relayed = q_all.at[u, 1 - zh]
    to_peers("q_second", lambda v: (relayed, relayed))
    landed("kv_far", kv_mine)
    kv_relayed = kv_all.at[core, y, z_far]
    start("kv_second", kv_relayed, kv_relayed, near)
    start("kv_row", kv_relayed, kv_relayed, across)
    start_t(1)

    row_at = lax.rem(lax.broadcasted_iota(jnp.int32, (n * owned, n * owned), 0), owned)
    col_at = lax.rem(lax.broadcasted_iota(jnp.int32, (n * owned, n * owned), 1), owned)
    same = row_at == col_at

    def temporal(i):
        landed(f"temporal{i}", t_recv.at[i])
        q, k_, v = (t_recv[i, :, t].reshape(n * owned, hd) for t in range(3))
        _, total, summed = attend(q, k_, v, same, scale)
        o_send[i] = (summed / total).astype(bf16).reshape(n, owned, hd)
        dst = o_recv.at[third * core + i, chip]
        keep("attended", o_send.at[i, me], dst)

        def go(k, c):
            to = lax.rem(me + k, n)
            start("attended", o_send.at[i, to], dst, to)
            return c

        lax.fori_loop(1, n, go, 0)

    landed("q_row", q_all.at[0:2, 0])
    landed("pair_video", pair_video)
    landed("pair_text", pair_text)

    length = len_ref[0]
    key = lax.broadcasted_iota(jnp.int32, (1, 2 * positions + 2 * shard), 1)
    offset = key - 2 * positions
    token = jnp.where(offset < shard, me * shard + offset, partner * shard + offset - shard)
    key_ok = (offset < 0) | (token < length)
    rows = 4 * shard
    lane = lax.broadcasted_iota(jnp.int32, (rows, 128), 1)

    def coded(logs):
        at = lax.broadcasted_iota(jnp.int32, logs.shape, 1)
        high = logs.astype(bf16).astype(f32)
        middle = (logs - high).astype(bf16).astype(f32)
        low = logs - high - middle
        return jnp.where(
            at < 16, high, jnp.where(at < 32, pltpu.roll(middle, 16, 1), pltpu.roll(low, 32, 1))
        ).astype(bf16)

    def decoded(code):
        code = code.astype(f32)
        return code + pltpu.roll(code, 112, 1) + pltpu.roll(code, 96, 1)

    def partial(side):
        tops = jnp.zeros((rows, 128), f32)
        sums = jnp.ones((rows, 128), f32)
        for h in range(heads):
            hs = slice(h * hd, (h + 1) * hd)
            q = q_all[:, side, :, hs].reshape(rows, hd)
            keys, values = (
                jnp.concatenate(
                    [video_ref[t + 1, h], pair_video[t, :, hs], text_ref[t + 1, h], pair_text[t, :, hs]],
                    axis=0,
                )
                for t in range(2)
            )
            top, total, summed = attend(q, keys, values, key_ok, scale)
            p_send[:, side, :, hs] = (summed / total).astype(bf16).reshape(4, shard, hd)
            tops = jnp.where(lane == h, top, tops)
            sums = jnp.where(lane == h, total, sums)
        logs = coded(tops * scale + jnp.log(sums) * log2_e)
        p_send[:, side, :, width:] = logs.reshape(4, shard, 128)

    def give(name, side):
        keep(name, p_send.at[u, side], p_recv.at[u, side])
        to_peers(name, lambda v: (p_send.at[v, side], p_recv.at[u, side]))

    partial(zh)
    for v in range(2):
        start("part_row", p_send.at[2 * v + 1 - y, zh], p_mid.at[v], across)

    landed("q_second", q_all.at[0:3, 0])
    partial(1 - zh)
    give("part", 1 - zh)
    start_t(2)
    temporal(0)

    landed("kv_first", kv_mine)
    landed("kv_second", kv_mine)
    for slot in (z_near, lax.rem(z_near + 2, 4)):
        block = kv_all.at[core, y, slot]
        start("kv_row", block, block, across)
    column = kv_all.at[core, y]
    start("kv_own", column, column, partner)

    def combine(parts):
        logs = [decoded(p[:, width:]) for p in parts]
        best = functools.reduce(jnp.maximum, logs)
        weights = [jnp.exp2(jnp.minimum(log - best, 0.0)) for log in logs]
        total = functools.reduce(jnp.add, weights)
        weights = [w / total for w in weights]
        blocks = []
        for h in range(heads):
            hs = slice(h * hd, (h + 1) * hd)
            terms = [w[:, h : h + 1] * p[:, hs].astype(f32) for w, p in zip(weights, parts)]
            blocks.append(functools.reduce(jnp.add, terms).astype(bf16))
        return blocks, best + jnp.log(total) * log2_e


    temporal(1)

    landed("part", p_recv.at[:, 0])
    blocks, logs = combine([p_recv[v, 1 - zh] for v in range(4)])
    for h in range(heads):
        p_out[:, h * hd : (h + 1) * hd] = blocks[h]
    p_out[:, width:] = coded(logs)
    start("part_far", p_out, p_far, far)

    temporal(2)
    landed("part_row", p_mid)
    ours_row = jnp.concatenate([p_send[y, zh], p_send[2 + y, zh]], axis=0)
    blocks, logs = combine([ours_row, p_mid[...].reshape(2 * shard, width + 128)])
    for h in range(heads):
        p_own[:, :, h * hd : (h + 1) * hd] = blocks[h].reshape(2, shard, hd)
    p_own[:, :, width:] = coded(logs).reshape(2, shard, 128)
    start("part_own", p_own.at[1 - lax.rem(z, 2)], p_near, near)

    landed("kv_row", column)
    ours = kv_all.at[core, 1 - y]
    start("kv_core", ours, ours, partner)
    landed("kv_own", column)

    landed("kv_core", ours)
    at = lax.broadcasted_iota(jnp.int32, (1, positions + n * shard), 1) - positions
    block = jnp.maximum(at, 0) // shard
    source = lax.rem(block, 4) * 4 + lax.rem(block // 4, 2) * 2 + block // 8
    joint_ok = (at < 0) | (source * shard + lax.rem(jnp.maximum(at, 0), shard) < length)
    for i in range(half):
        hs = slice(i * hd, (i + 1) * hd)
        keys, values = (
            jnp.concatenate(
                [video_ref[t + 1, head_ref[i]], kv_all[:, :, :, t, :, hs].reshape(n * shard, hd)],
                axis=0,
            )
            for t in range(2)
        )
        _, total, summed = attend(video_ref[0, head_ref[i]], keys, values, joint_ok, scale)
        result[i] = (summed / total).astype(bf16)

    landed("part_own", p_near)
    landed("part_far", p_out)
    blocks, _ = combine([p_own[lax.rem(z, 2)], p_near[...], p_far[...]])
    for h in range(heads):
        text_out[:, h * hd : (h + 1) * hd] = blocks[h]

    landed("attended", o_recv)
    for h in range(heads):
        spatial = result[jnp.minimum(place_ref[h], half - 1)]
        temporal_block = o_recv[jnp.maximum(place_ref[h] - half, 0)].reshape(positions, hd)
        video_out[:, h * hd : (h + 1) * hd] = jnp.where(place_ref[h] < half, spatial, temporal_block)

    sent("pair_video", pair_video)
    sent("pair_text", pair_text)
    sent("q_far", mine)
    sent("q_first", mine)
    sent("q_row", q_all.at[0:2, 0])
    sent("q_second", q_all.at[0:3, 0])
    sent("kv_far", kv_mine)
    sent("kv_first", kv_mine)
    sent("kv_second", kv_mine)
    sent("kv_row", column)
    sent("kv_core", ours)
    sent("kv_own", column)
    sent("part", p_send.at[0:3, 0])
    sent("part_row", p_mid)
    sent("part_own", p_near)
    sent("part_far", p_out)
    for i in range(3):
        sent(f"temporal{i}", t_recv.at[i, 0 : n - 1])
    sent("attended", o_send.at[:, 0 : n - 1])


def hand_over(video, text, video_out, text_out, sem):
    copies = [
        pltpu.make_async_copy(video, video_out, sem.at[0]),
        pltpu.make_async_copy(text, text_out, sem.at[1]),
    ]
    for copy in copies:
        copy.start()
    for copy in copies:
        copy.wait()


def fused_body(video_qkv, text_qkv, head_kind, text_len):
    heads = head_kind.shape[0]
    _, _, positions, width = video_qkv.shape
    shard = text_qkv.shape[1]
    n, half, hd = 16, heads // 2, width // heads
    owned, narrow, coded = positions // 8, half * hd, width + 128
    vmem = pl.BlockSpec(memory_space=pltpu.VMEM)
    hbm = pl.BlockSpec(memory_space=pltpu.HBM)
    dma = pltpu.SemaphoreType.DMA
    kind, video, words = (
        pltpu.with_memory_space_constraint(a, pltpu.HBM)
        for a in (head_kind, video_qkv.reshape(3, positions, width), text_qkv)
    )
    held = pl.pallas_call(
        functools.partial(kernel, heads),
        out_shape=(
            pltpu.VMEM((positions, width), bf16),
            pltpu.VMEM((shard, width), bf16),
        ),
        in_specs=[hbm] * 4,
        out_specs=(vmem, vmem),
        scratch_shapes=[
            pltpu.SMEM((heads,), jnp.int32),
            pltpu.SMEM((1,), jnp.int32),
            pltpu.SMEM((heads,), jnp.int32),
            pltpu.SMEM((heads,), jnp.int32),
            pltpu.VMEM((3, heads, positions, hd), bf16),
            pltpu.VMEM((3, heads, shard, hd), bf16),
            pltpu.VMEM((2, positions, width), bf16),
            pltpu.VMEM((2, shard, width), bf16),
            pltpu.VMEM((4, 2, shard, width), bf16),
            pltpu.VMEM((2, 2, 4, 2, shard, narrow), bf16),
            pltpu.VMEM((3, 8, 2, 3, owned, hd), bf16),
            pltpu.VMEM((3, n, 3, owned, hd), bf16),
            pltpu.VMEM((3, n, owned, hd), bf16),
            pltpu.VMEM((half, 8, owned, hd), bf16),
            pltpu.VMEM((4, 2, shard, coded), bf16),
            pltpu.VMEM((4, 2, shard, coded), bf16),
            pltpu.VMEM((2, shard, coded), bf16),
            pltpu.VMEM((2, shard, coded), bf16),
            pltpu.VMEM((shard, coded), bf16),
            pltpu.VMEM((shard, coded), bf16),
            pltpu.VMEM((shard, coded), bf16),
            pltpu.VMEM((half, positions, hd), bf16),
            dma((4,)),
            dma((len(names),)),
            dma((len(names),)),
        ],
        compiler_params=pltpu.CompilerParams(
            collective_id=0, has_side_effects=True, vmem_limit_bytes=24 << 20
        ),
    )(kind, text_len, video, words)
    video_out, text_out = pl.pallas_call(
        hand_over,
        out_shape=(
            jax.ShapeDtypeStruct((positions, width), bf16),
            jax.ShapeDtypeStruct((shard, width), bf16),
        ),
        in_specs=[vmem, vmem],
        out_specs=(hbm, hbm),
        scratch_shapes=[dma((2,))],
        compiler_params=pltpu.CompilerParams(vmem_limit_bytes=8 << 20),
    )(*held)
    return video_out.reshape(1, positions, width), text_out


def body(n, video_qkv, text_qkv, head_kind, text_len):
    heads = head_kind.shape[0]
    positions, width = video_qkv.shape[2:]
    shard = text_qkv.shape[1]
    whole_tiles = (
        video_qkv.shape[1] == 1
        and n == 16
        and heads == 12
        and shard % 16 == 0
        and positions % 128 == 0
        and width == heads * 128
    )
    if whole_tiles:
        return fused_body(video_qkv, text_qkv, head_kind, text_len)
    return plain_body(video_qkv, text_qkv, head_kind, text_len)


def solution(mesh):
    in_specs = (
        P(None, ("groups", "frame"), None, None),
        P(None, ("groups", "frame"), None),
        P("groups"),
        P("groups"),
    )
    out_specs = (P(("groups", "frame"), None, None), P(("groups", "frame"), None))
    return jax.shard_map(
        functools.partial(body, mesh.shape["frame"]),
        mesh=mesh,
        in_specs=in_specs,
        out_specs=out_specs,
        check_vma=False,
    )
```

```python
import functools

import jax
import jax.numpy as jnp
import numpy as np
from jax import lax
from jax.experimental import pallas as pl
from jax.experimental.pallas import tpu as pltpu
from jax.sharding import PartitionSpec as P

masked_score = -1e30
log2_e = float(np.log2(np.e))
f32 = jnp.float32
bf16 = jnp.bfloat16


def pick(one_hot, array, dims):
    return jnp.einsum(dims, one_hot, array, preferred_element_type=f32).astype(bf16)


def plain_body(video_qkv, text_qkv, head_kind, text_len):
    head_count = head_kind.shape[0]
    head_width = video_qkv.shape[-1]
    head_dim = head_width // head_count
    positions = video_qkv.shape[2]
    shard_text = text_qkv.shape[1]
    half = head_count // 2
    score_scale = head_dim ** (-0.5)
    device_rank = lax.axis_index("frame")
    local_video = video_qkv.reshape(3, 1, positions, head_count, head_dim)
    gathered = lax.all_gather(text_qkv, "frame", axis=1, tiled=True)
    text_total = gathered.shape[1]
    all_text = gathered.reshape(3, text_total, head_count, head_dim)
    text_valid = jnp.arange(text_total) < text_len[0]
    head_at = jnp.arange(head_count)
    earlier = head_at[None, :] < head_at[:, None]
    same_kind = head_kind[None, :] == head_kind[:, None]
    rank = jnp.sum(jnp.where(earlier & same_kind, 1, 0), axis=1)
    place = rank + half * head_kind
    slots = (place[None, :] == head_at[:, None]).astype(bf16)
    spatial, temporal = slots[:half], slots[half:]
    own_frame = pick(spatial, local_video[:, 0], "ih,tphd->tpid")
    text_spatial = pick(spatial, all_text[1:], "ih,tphd->tpid")
    joint_keys = jnp.concatenate([own_frame[1], text_spatial[0]], axis=0)
    joint_values = jnp.concatenate([own_frame[2], text_spatial[1]], axis=0)
    joint_valid = jnp.concatenate([jnp.ones((positions,), bool), text_valid])
    spatial_scores = (
        jnp.einsum("phd,khd->hpk", own_frame[0], joint_keys, preferred_element_type=f32)
        * score_scale
    )
    spatial_scores = jnp.where(joint_valid, spatial_scores, masked_score)
    row_max = spatial_scores.max(-1, keepdims=True)
    spatial_exp = jnp.exp(spatial_scores - row_max)
    totals = spatial_exp.sum(-1)
    summed = jnp.einsum(
        "hpk,khd->phd", spatial_exp.astype(bf16), joint_values, preferred_element_type=f32
    )
    spatial_result = (summed / totals.T[..., None]).astype(bf16)
    selected = pick(temporal, local_video, "ih,tfphd->tfpid")
    block = lax.all_to_all(selected, "frame", split_axis=2, concat_axis=1, tiled=True)
    scores = (
        jnp.einsum("fphd,gphd->phfg", block[0], block[1], preferred_element_type=f32) * score_scale
    )
    block_max = scores.max(-1, keepdims=True)
    exps = jnp.exp(scores - block_max)
    block_totals = exps.sum(-1)
    block_sum = jnp.einsum(
        "phfg,gphd->fphd", exps.astype(bf16), block[2], preferred_element_type=f32
    )
    result = (block_sum / jnp.transpose(block_totals, (2, 0, 1))[..., None]).astype(bf16)
    temporal_result = lax.all_to_all(result, "frame", split_axis=0, concat_axis=1, tiled=True)[0]
    joined = jnp.concatenate([spatial_result, temporal_result], axis=1)
    video_out = pick(slots, joined, "ih,pid->phd").reshape(1, positions, head_width)
    text_queries = all_text[0]
    own_text = text_qkv.reshape(3, shard_text, head_count, head_dim)
    own_valid = device_rank * shard_text + jnp.arange(shard_text) < text_len[0]
    local_keys = jnp.concatenate([local_video[1, 0], own_text[1]], axis=0)
    local_values = jnp.concatenate([local_video[2, 0], own_text[2]], axis=0)
    local_valid = jnp.concatenate([jnp.ones((positions,), bool), own_valid])
    query_scores = (
        jnp.einsum("thd,khd->thk", text_queries, local_keys, preferred_element_type=f32)
        * score_scale
    )
    query_scores = jnp.where(local_valid, query_scores, masked_score)
    local_max = query_scores.max(-1)
    global_max = lax.pmax(local_max, "frame")
    query_exp = jnp.exp(query_scores - global_max[..., None])
    query_totals = query_exp.sum(-1)
    query_sums = jnp.einsum(
        "thk,khd->thd", query_exp.astype(bf16), local_values, preferred_element_type=f32
    )
    query_sums = lax.psum_scatter(query_sums, "frame", scatter_dimension=0, tiled=True)
    query_totals = lax.psum_scatter(query_totals, "frame", scatter_dimension=0, tiled=True)
    text_out = (query_sums / query_totals[..., None]).astype(bf16).reshape(shard_text, head_width)
    return (video_out, text_out)


def dot_nt(a, b):
    return lax.dot_general(a, b, (((1,), (1,)), ((), ())), preferred_element_type=f32)


def dot_nn(a, b):
    return lax.dot_general(a, b, (((1,), (0,)), ((), ())), preferred_element_type=f32)


def attend(q, keys, values, ok, scale):
    s = jnp.where(ok, dot_nt(q, keys), masked_score)
    top = s.max(-1, keepdims=True)
    w = jnp.exp2((s - top) * scale).astype(bf16)
    hd = values.shape[1]
    both = dot_nn(w, jnp.concatenate([values, jnp.ones_like(values)], axis=1))
    return top, both[:, hd:], both[:, :hd]


def remote(src, dst, send_sem, recv_sem, peer):
    return pltpu.make_async_remote_copy(
        src_ref=src,
        dst_ref=dst,
        send_sem=send_sem,
        recv_sem=recv_sem,
        device_id={"frame": peer},
        device_id_type=pl.DeviceIdType.MESH,
    )


names = (
    "pair_video",
    "pair_text",
    "q_far",
    "q_first",
    "q_second",
    "q_row",
    "kv_far",
    "kv_first",
    "kv_second",
    "kv_row",
    "kv_core",
    "kv_own",
    "part",
    "part_row",
    "part_own",
    "part_far",
    "attended",
    "temporal0",
    "temporal1",
    "temporal2",
)
sem_at = {name: i for i, name in enumerate(names)}


def kernel(
    heads,
    kind_hbm,
    len_hbm,
    video_hbm,
    text_hbm,
    video_out,
    text_out,
    kind_ref,
    len_ref,
    head_ref,
    place_ref,
    video_ref,
    text_ref,
    pair_video,
    pair_text,
    q_all,
    kv_all,
    t_send,
    t_recv,
    o_send,
    o_recv,
    p_send,
    p_recv,
    p_mid,
    p_own,
    p_near,
    p_out,
    p_far,
    result,
    in_sem,
    send_sem,
    recv_sem,
):
    n = 16
    half = heads // 2
    third = half // 2
    positions, hd = video_ref.shape[2:]
    shard = text_ref.shape[2]
    width = heads * hd
    owned = positions // 8
    scale = hd ** (-0.5) * log2_e
    me = lax.axis_index("frame")
    core = lax.rem(me, 2)
    y = lax.rem(me // 2, 2)
    z = me // 4
    u = lax.rem(me // 2, 4)
    zh = me // 8
    chip = me // 2
    far = lax.rem(me + 8, n)
    z_near = z + 1 - 2 * lax.rem(z, 2)
    z_far = lax.rem(z + 2, 4)
    near = z_near * 4 + y * 2 + core
    across = me + 2 - 4 * y
    partner = me + 1 - 2 * core

    barrier = pltpu.get_barrier_semaphore()

    def greet(k, c):
        pl.semaphore_signal(
            barrier,
            inc=1,
            device_id={"frame": lax.rem(me + k, n)},
            device_id_type=pl.DeviceIdType.MESH,
        )
        return c

    lax.fori_loop(1, n, greet, 0)
    pltpu.make_async_copy(kind_hbm, kind_ref, in_sem.at[0]).start()
    pltpu.make_async_copy(len_hbm, len_ref, in_sem.at[1]).start()
    for src, dst, i in ((text_hbm, text_ref, 2), (video_hbm, video_ref, 3)):
        for h in range(heads):
            hs = slice(h * hd, (h + 1) * hd)
            pltpu.make_async_copy(src.at[:, :, hs], dst.at[:, h], in_sem.at[i]).start()
    def prepare():
        for i, ref in enumerate((kind_ref, len_ref, text_ref)):
            pltpu.make_async_copy(ref, ref, in_sem.at[i]).wait()
        seen = [jnp.int32(0), jnp.int32(0)]
        places = []
        for h in range(heads):
            kind = kind_ref[h]
            places.append(jnp.where(kind == 0, seen[0], half + seen[1]))
            place_ref[h] = places[h]
            seen[0] = seen[0] + jnp.where(kind == 0, 1, 0)
            seen[1] = seen[1] + jnp.where(kind == 0, 0, 1)
        head_in = []
        for i in range(heads):
            first = i % half
            head = jnp.int32(first)
            for h in range(first + 1, first + half + 1):
                head = jnp.where(places[h] == i, h, head)
            head_ref[i] = head
            head_in.append(head)
        for i in range(half):
            for t in range(2):
                kv_all[core, y, z, t, :, i * hd : (i + 1) * hd] = text_ref[t + 1, head_in[i]]
        for h in range(heads):
            q_all[u, zh, :, h * hd : (h + 1) * hd] = text_ref[0, h]
        pltpu.make_async_copy(video_ref, video_ref, in_sem.at[3]).wait()
        for i in range(3):
            for k in range(2):
                for t in range(3):
                    block = video_ref[t, head_in[half + third * k + i]].reshape(8, owned, hd)
                    t_send[i, :, k, t] = block

    def start(name, src, dst, to):
        i = sem_at[name]
        remote(src, dst, send_sem.at[i], recv_sem.at[i], to).start()

    def keep(name, src, dst):
        pltpu.make_async_copy(src, dst, recv_sem.at[sem_at[name]]).start()

    def landed(name, like):
        i = sem_at[name]
        remote(like, like, send_sem.at[i], recv_sem.at[i], partner).wait_recv()

    def sent(name, like):
        i = sem_at[name]
        remote(like, like, send_sem.at[i], recv_sem.at[i], partner).wait_send()

    def to_peers(name, block_of):
        def go(k, c):
            v = lax.rem(u + k, 4)
            src, dst = block_of(v)
            start(name, src, dst, zh * 8 + v * 2 + core)
            return c

        lax.fori_loop(1, 4, go, 0)

    early = z < 2
    pl.when(early)(prepare)

    pl.semaphore_wait(barrier, n - 1)

    mine = q_all.at[u, zh]
    words = text_hbm.at[0]
    start("q_far", words, mine, far)
    start("q_first", words, mine, near)
    start("q_row", words, mine, across)
    start("pair_video", video_hbm.at[1:3], pair_video, partner)
    start("pair_text", text_hbm.at[1:3], pair_text, partner)

    pl.when(jnp.logical_not(early))(prepare)

    kv_mine = kv_all.at[core, y, z]
    start("kv_far", kv_mine, kv_mine, far)

    def start_t(i):
        name = f"temporal{i}"
        keep(name, t_send.at[i, chip, core], t_recv.at[i, me])

        def go(k, c):
            to = lax.rem(me + lax.rem(k + 10, 15) + 1, n)
            start(name, t_send.at[i, to // 2, lax.rem(to, 2)], t_recv.at[i, me], to)
            return c

        lax.fori_loop(1, n, go, 0)

    start_t(0)
    start("kv_first", kv_mine, kv_mine, near)
    start("kv_row", kv_mine, kv_mine, across)

    landed("q_first", mine)
    q_near = q_all.at[lax.rem(u + 2, 4), zh]
    start("q_row", q_near, q_near, across)
    landed("q_far", mine)
    relayed = q_all.at[u, 1 - zh]
    to_peers("q_second", lambda v: (relayed, relayed))
    landed("kv_far", kv_mine)
    kv_relayed = kv_all.at[core, y, z_far]
    start("kv_second", kv_relayed, kv_relayed, near)
    start("kv_row", kv_relayed, kv_relayed, across)
    start_t(1)

    row_at = lax.rem(lax.broadcasted_iota(jnp.int32, (n * owned, n * owned), 0), owned)
    col_at = lax.rem(lax.broadcasted_iota(jnp.int32, (n * owned, n * owned), 1), owned)
    same = row_at == col_at

    def temporal(i):
        landed(f"temporal{i}", t_recv.at[i])
        q, k_, v = (t_recv[i, :, t].reshape(n * owned, hd) for t in range(3))
        _, total, summed = attend(q, k_, v, same, scale)
        o_send[i] = (summed / total).astype(bf16).reshape(n, owned, hd)
        dst = o_recv.at[third * core + i, chip]
        keep("attended", o_send.at[i, me], dst)

        def go(k, c):
            to = lax.rem(me + k, n)
            start("attended", o_send.at[i, to], dst, to)
            return c

        lax.fori_loop(1, n, go, 0)

    landed("q_row", q_all.at[0:2, 0])
    landed("pair_video", pair_video)
    landed("pair_text", pair_text)

    length = len_ref[0]
    key = lax.broadcasted_iota(jnp.int32, (1, 2 * positions + 2 * shard), 1)
    offset = key - 2 * positions
    token = jnp.where(offset < shard, me * shard + offset, partner * shard + offset - shard)
    key_ok = (offset < 0) | (token < length)
    rows = 4 * shard
    lane = lax.broadcasted_iota(jnp.int32, (rows, 128), 1)

    def coded(logs):
        at = lax.broadcasted_iota(jnp.int32, logs.shape, 1)
        high = logs.astype(bf16).astype(f32)
        middle = (logs - high).astype(bf16).astype(f32)
        low = logs - high - middle
        return jnp.where(
            at < 16, high, jnp.where(at < 32, pltpu.roll(middle, 16, 1), pltpu.roll(low, 32, 1))
        ).astype(bf16)

    def decoded(code):
        code = code.astype(f32)
        return code + pltpu.roll(code, 112, 1) + pltpu.roll(code, 96, 1)

    def partial(side):
        tops = jnp.zeros((rows, 128), f32)
        sums = jnp.ones((rows, 128), f32)
        for h in range(heads):
            hs = slice(h * hd, (h + 1) * hd)
            q = q_all[:, side, :, hs].reshape(rows, hd)
            keys, values = (
                jnp.concatenate(
                    [video_ref[t + 1, h], pair_video[t, :, hs], text_ref[t + 1, h], pair_text[t, :, hs]],
                    axis=0,
                )
                for t in range(2)
            )
            top, total, summed = attend(q, keys, values, key_ok, scale)
            p_send[:, side, :, hs] = (summed / total).astype(bf16).reshape(4, shard, hd)
            tops = jnp.where(lane == h, top, tops)
            sums = jnp.where(lane == h, total, sums)
        logs = coded(tops * scale + jnp.log(sums) * log2_e)
        p_send[:, side, :, width:] = logs.reshape(4, shard, 128)

    def give(name, side):
        keep(name, p_send.at[u, side], p_recv.at[u, side])
        to_peers(name, lambda v: (p_send.at[v, side], p_recv.at[u, side]))

    partial(zh)
    for v in range(2):
        start("part_row", p_send.at[2 * v + 1 - y, zh], p_mid.at[v], across)

    landed("q_second", q_all.at[0:3, 0])
    partial(1 - zh)
    give("part", 1 - zh)
    start_t(2)
    temporal(0)

    landed("kv_first", kv_mine)
    landed("kv_second", kv_mine)
    for slot in (z_near, lax.rem(z_near + 2, 4)):
        block = kv_all.at[core, y, slot]
        start("kv_row", block, block, across)
    column = kv_all.at[core, y]
    start("kv_own", column, column, partner)

    def combine(parts):
        logs = [decoded(p[:, width:]) for p in parts]
        best = functools.reduce(jnp.maximum, logs)
        weights = [jnp.exp2(jnp.minimum(log - best, 0.0)) for log in logs]
        total = functools.reduce(jnp.add, weights)
        weights = [w / total for w in weights]
        blocks = []
        for h in range(heads):
            hs = slice(h * hd, (h + 1) * hd)
            terms = [w[:, h : h + 1] * p[:, hs].astype(f32) for w, p in zip(weights, parts)]
            blocks.append(functools.reduce(jnp.add, terms).astype(bf16))
        return blocks, best + jnp.log(total) * log2_e


    temporal(1)

    landed("part", p_recv.at[:, 0])
    blocks, logs = combine([p_recv[v, 1 - zh] for v in range(4)])
    for h in range(heads):
        p_out[:, h * hd : (h + 1) * hd] = blocks[h]
    p_out[:, width:] = coded(logs)
    start("part_far", p_out, p_far, far)

    temporal(2)
    landed("part_row", p_mid)
    ours_row = jnp.concatenate([p_send[y, zh], p_send[2 + y, zh]], axis=0)
    blocks, logs = combine([ours_row, p_mid[...].reshape(2 * shard, width + 128)])
    for h in range(heads):
        p_own[:, :, h * hd : (h + 1) * hd] = blocks[h].reshape(2, shard, hd)
    p_own[:, :, width:] = coded(logs).reshape(2, shard, 128)
    start("part_own", p_own.at[1 - lax.rem(z, 2)], p_near, near)

    landed("kv_row", column)
    ours = kv_all.at[core, 1 - y]
    start("kv_core", ours, ours, partner)
    landed("kv_own", column)

    landed("kv_core", ours)
    at = lax.broadcasted_iota(jnp.int32, (1, positions + n * shard), 1) - positions
    block = jnp.maximum(at, 0) // shard
    source = lax.rem(block, 4) * 4 + lax.rem(block // 4, 2) * 2 + block // 8
    joint_ok = (at < 0) | (source * shard + lax.rem(jnp.maximum(at, 0), shard) < length)
    for i in range(half):
        hs = slice(i * hd, (i + 1) * hd)
        keys, values = (
            jnp.concatenate(
                [video_ref[t + 1, head_ref[i]], kv_all[:, :, :, t, :, hs].reshape(n * shard, hd)],
                axis=0,
            )
            for t in range(2)
        )
        _, total, summed = attend(video_ref[0, head_ref[i]], keys, values, joint_ok, scale)
        result[i] = (summed / total).astype(bf16)

    landed("part_own", p_near)
    landed("part_far", p_out)
    blocks, _ = combine([p_own[lax.rem(z, 2)], p_near[...], p_far[...]])
    for h in range(heads):
        text_out[:, h * hd : (h + 1) * hd] = blocks[h]

    landed("attended", o_recv)
    for h in range(heads):
        spatial = result[jnp.minimum(place_ref[h], half - 1)]
        temporal_block = o_recv[jnp.maximum(place_ref[h] - half, 0)].reshape(positions, hd)
        video_out[:, h * hd : (h + 1) * hd] = jnp.where(place_ref[h] < half, spatial, temporal_block)

    sent("pair_video", pair_video)
    sent("pair_text", pair_text)
    sent("q_far", mine)
    sent("q_first", mine)
    sent("q_row", q_all.at[0:2, 0])
    sent("q_second", q_all.at[0:3, 0])
    sent("kv_far", kv_mine)
    sent("kv_first", kv_mine)
    sent("kv_second", kv_mine)
    sent("kv_row", column)
    sent("kv_core", ours)
    sent("kv_own", column)
    sent("part", p_send.at[0:3, 0])
    sent("part_row", p_mid)
    sent("part_own", p_near)
    sent("part_far", p_out)
    for i in range(3):
        sent(f"temporal{i}", t_recv.at[i, 0 : n - 1])
    sent("attended", o_send.at[:, 0 : n - 1])


def hand_over(video, text, video_out, text_out, sem):
    copies = [
        pltpu.make_async_copy(video, video_out, sem.at[0]),
        pltpu.make_async_copy(text, text_out, sem.at[1]),
    ]
    for copy in copies:
        copy.start()
    for copy in copies:
        copy.wait()


def fused_body(video_qkv, text_qkv, head_kind, text_len):
    heads = head_kind.shape[0]
    _, _, positions, width = video_qkv.shape
    shard = text_qkv.shape[1]
    n, half, hd = 16, heads // 2, width // heads
    owned, narrow, coded = positions // 8, half * hd, width + 128
    vmem = pl.BlockSpec(memory_space=pltpu.VMEM)
    hbm = pl.BlockSpec(memory_space=pltpu.HBM)
    dma = pltpu.SemaphoreType.DMA
    kind, video, words = (
        pltpu.with_memory_space_constraint(a, pltpu.HBM)
        for a in (head_kind, video_qkv.reshape(3, positions, width), text_qkv)
    )
    held = pl.pallas_call(
        functools.partial(kernel, heads),
        out_shape=(
            pltpu.VMEM((positions, width), bf16),
            pltpu.VMEM((shard, width), bf16),
        ),
        in_specs=[hbm] * 4,
        out_specs=(vmem, vmem),
        scratch_shapes=[
            pltpu.SMEM((heads,), jnp.int32),
            pltpu.SMEM((1,), jnp.int32),
            pltpu.SMEM((heads,), jnp.int32),
            pltpu.SMEM((heads,), jnp.int32),
            pltpu.VMEM((3, heads, positions, hd), bf16),
            pltpu.VMEM((3, heads, shard, hd), bf16),
            pltpu.VMEM((2, positions, width), bf16),
            pltpu.VMEM((2, shard, width), bf16),
            pltpu.VMEM((4, 2, shard, width), bf16),
            pltpu.VMEM((2, 2, 4, 2, shard, narrow), bf16),
            pltpu.VMEM((3, 8, 2, 3, owned, hd), bf16),
            pltpu.VMEM((3, n, 3, owned, hd), bf16),
            pltpu.VMEM((3, n, owned, hd), bf16),
            pltpu.VMEM((half, 8, owned, hd), bf16),
            pltpu.VMEM((4, 2, shard, coded), bf16),
            pltpu.VMEM((4, 2, shard, coded), bf16),
            pltpu.VMEM((2, shard, coded), bf16),
            pltpu.VMEM((2, shard, coded), bf16),
            pltpu.VMEM((shard, coded), bf16),
            pltpu.VMEM((shard, coded), bf16),
            pltpu.VMEM((shard, coded), bf16),
            pltpu.VMEM((half, positions, hd), bf16),
            dma((4,)),
            dma((len(names),)),
            dma((len(names),)),
        ],
        compiler_params=pltpu.CompilerParams(
            collective_id=0, has_side_effects=True, vmem_limit_bytes=24 << 20
        ),
    )(kind, text_len, video, words)
    video_out, text_out = pl.pallas_call(
        hand_over,
        out_shape=(
            jax.ShapeDtypeStruct((positions, width), bf16),
            jax.ShapeDtypeStruct((shard, width), bf16),
        ),
        in_specs=[vmem, vmem],
        out_specs=(hbm, hbm),
        scratch_shapes=[dma((2,))],
        compiler_params=pltpu.CompilerParams(vmem_limit_bytes=8 << 20),
    )(*held)
    return video_out.reshape(1, positions, width), text_out


def body(n, video_qkv, text_qkv, head_kind, text_len):
    heads = head_kind.shape[0]
    positions, width = video_qkv.shape[2:]
    shard = text_qkv.shape[1]
    whole_tiles = (
        video_qkv.shape[1] == 1
        and n == 16
        and heads == 12
        and shard % 16 == 0
        and positions % 128 == 0
        and width == heads * 128
    )
    if whole_tiles:
        return fused_body(video_qkv, text_qkv, head_kind, text_len)
    return plain_body(video_qkv, text_qkv, head_kind, text_len)


def solution(mesh):
    in_specs = (
        P(None, ("groups", "frame"), None, None),
        P(None, ("groups", "frame"), None),
        P("groups"),
        P("groups"),
    )
    out_specs = (P(("groups", "frame"), None, None), P(("groups", "frame"), None))
    return jax.shard_map(
        functools.partial(body, mesh.shape["frame"]),
        mesh=mesh,
        in_specs=in_specs,
        out_specs=out_specs,
        check_vma=False,
    )
```
